256 devices in a mesh: row: 8 (over z), col: 32 (over x, y, core).
Axes of the slice: x: 4, y: 4, z: 8, core: 2. Of those that a mesh axis runs over, the one named last changes fastest.
Arguments:
- tile_data: bfloat16 [8, 32, 32, 256, 256], P('row', 'col'), may hold values from -0.125 to 0.125
- tile_row_block: int32 [8, 32, 32], P('row', 'col'), may hold values from 0 to 63
- tile_column_block: int32 [8, 32, 32], P('row', 'col'), may hold values from 0 to 63
- tile_count: int32 [8, 32], P('row', 'col'), may hold values from 1 to 32, as said below
- saved_primal: float32 [3, 524288], P(None, 'col'), may hold values from 0 to 1
- saved_dual: float32 [3, 131072], P(None, 'row'), may hold values from 0 to 1
- primal_mask: int32 [3, 524288], P(None, 'col'), may hold values 0 or 1
- dual_mask: int32 [3, 131072], P(None, 'row'), may hold values 0 or 1
- cost_vector: float32 [524288], P('col'), may hold values from -6 to 6
- demand: float32 [131072], P('row'), may hold values from -6 to 6
- upper_bound: float32 [524288], P('col'), may hold values from 0.5 to 1.5
- step_sizes: float32 [2], replicated, may hold values from 0.2 to 0.4
- primal_cotangent: float32 [524288], P('col'), may hold values from -6 to 6
- dual_cotangent: float32 [131072], P('row'), may hold values from -6 to 6
Outputs:
- primal_adjoint: float32 [524288], P('col')
- dual_adjoint: float32 [131072], P(('row', 'col'))
- step_gradients: float32 [2], replicated
The draws below stay inside these ranges and needn't reach their ends.
Inputs may be any that keep to these rules, and one draw needn't show every extreme that they name: `tile_count`: block positions may repeat, and tiles at one position add; slots at and beyond a device's count are ignored. In every index of row some device has 32 live slots.
All inputs are finite; a program needn't handle non-finite values. No bound on the sum of `primal_mask` or of `dual_mask` on one device may be relied on, other than what follows from the above.
Results may differ from the reference program's by a relative error of at most 0.00071.
Values may be sent and summed in bfloat16 or wider, within the bound.
A program may use at most 64 MiB of HBM per device.

```python
import math
import jax
import jax.numpy as jnp
from jax import lax

TILE = 256
RB_DEV = 64
CB_DEV = 64
TILES_DEV = 32
ITERS = 3
ROWS_DEV = 16384
COLS_DEV = 16384
NROW = 131072
NCOL = 524288
N_ROW = 8
N_COL = 32


def draw_tile_count(key, part):
    light_counts = jax.random.randint(key, (N_ROW, N_COL), 1, TILES_DEV // 2 + 1)
    heavy_place = jax.random.randint(jax.random.fold_in(key, 7), (N_ROW, 1), 0, N_COL)
    places = jnp.arange(N_COL)[None, :]
    return jnp.where(places == heavy_place, TILES_DEV, light_counts).astype(jnp.int32)


def plant(array, own_key, smallest, largest):
    spot = [jax.random.randint(jax.random.fold_in(own_key, axis), (), 0, length) for axis, length in enumerate(array.shape)]
    main_axis = array.shape.index(max(array.shape))
    beside = spot[:main_axis] + [(spot[main_axis] + 1) % array.shape[main_axis]] + spot[main_axis + 1:]
    return array.at[tuple(spot)].set(smallest).at[tuple(beside)].set(largest)


def levels(stream_key, dims, shards, smallest, largest):
    def one(axis_at, blocks):
        steps = jax.random.uniform(jax.random.fold_in(jax.random.fold_in(stream_key, 6), axis_at), (blocks,), jnp.float32, smallest / len(shards), largest / len(shards))
        return jnp.repeat(jnp.exp(steps), dims[axis_at] // blocks).reshape((-1,) + (1,) * (len(dims) - axis_at - 1))

    level = one(*shards[0])
    for cut in shards[1:]:
        level = level * one(*cut)
    return level


def centred(stream_key, extent, deviation, reach, shards=(), kind=jnp.bfloat16):
    factor_of = levels(stream_key, extent, shards, -0.22, 0.18) if shards else 1.0
    entries = jax.random.normal(stream_key, extent, jnp.float32) * deviation * factor_of
    return jnp.minimum(jnp.maximum(entries, -reach), reach).astype(kind)


def setup_inputs(seed: int = 0) -> dict:
    key_list = jax.random.split(jax.random.key(seed), 15)
    return {
        "tile_data": centred(key_list[0], (N_ROW, N_COL, TILES_DEV, TILE, TILE), (8 * TILE) ** -0.5, 0.125, ((0, 8), (1, 32))),
        "tile_row_block": plant(jax.random.randint(key_list[1], (N_ROW, N_COL, TILES_DEV), 0, RB_DEV), jax.random.fold_in(key_list[1], 1), 0, RB_DEV - 1).astype(jnp.int32),
        "tile_column_block": plant(jax.random.randint(key_list[2], (N_ROW, N_COL, TILES_DEV), 0, CB_DEV), jax.random.fold_in(key_list[2], 1), 0, CB_DEV - 1).astype(jnp.int32),
        "tile_count": draw_tile_count(jax.random.fold_in(key_list[14], 71), 0),
        "saved_primal": jnp.clip(1.0 * jax.random.uniform(key_list[4], (ITERS, NCOL), jnp.float32) ** levels(key_list[4], (ITERS, NCOL), ((1, 32),), -0.2, 0.2), 0.0, 1.0),
        "saved_dual": jnp.clip(1.0 * jax.random.uniform(key_list[5], (ITERS, NROW), jnp.float32) ** levels(key_list[5], (ITERS, NROW), ((1, 8),), -0.2, 0.2), 0.0, 1.0),
        "primal_mask": plant((jax.random.randint(key_list[6], (ITERS, NCOL), 0, 4) < 3).astype(jnp.int32), jax.random.fold_in(key_list[6], 1), 0, 1),
        "dual_mask": plant((jax.random.randint(key_list[7], (ITERS, NROW), 0, 2) < 1).astype(jnp.int32), jax.random.fold_in(key_list[7], 1), 0, 1),
        "cost_vector": centred(key_list[8], (NCOL,), 1.0, 6.0, ((0, 32),), jnp.float32),
        "demand": centred(key_list[9], (NROW,), 1.0, 6.0, ((0, 8),), jnp.float32),
        "upper_bound": jnp.clip(0.5 + 1.0 * jax.random.uniform(key_list[10], (NCOL,), jnp.float32) ** levels(key_list[10], (NCOL,), ((0, 32),), -0.2, 0.2), 0.5, 1.5),
        "step_sizes": jnp.clip(jnp.exp(jax.random.uniform(key_list[11], (2,), jnp.float32, math.log(0.2), math.log(0.4))), 0.2, 0.4),
        "primal_cotangent": centred(key_list[12], (NCOL,), 1.0, 6.0, ((0, 32),), jnp.float32),
        "dual_cotangent": centred(key_list[13], (NROW,), 1.0, 6.0, ((0, 8),), jnp.float32),
    }


def apply_tiles(tile_data, tile_row_block, tile_column_block, tile_count, vectors, transpose):
    devices = N_ROW * N_COL
    stacked = tile_data.reshape(devices, TILES_DEV, TILE, TILE)
    rows_flat = tile_row_block.reshape(devices, TILES_DEV)
    cols_flat = tile_column_block.reshape(devices, TILES_DEV)
    counts = tile_count.reshape(devices)
    batch = vectors.shape[0]

    def device_term(inputs):
        tiles_here, rows_here, cols_here, count_here, device = inputs
        grid_row = device // N_COL
        grid_column = device % N_COL
        if transpose:
            piece = lax.dynamic_slice_in_dim(vectors, (grid_row * ROWS_DEV).astype(jnp.int32), ROWS_DEV, 1)
            in_index, out_index, out_blocks = (rows_here, cols_here, CB_DEV)
            einsum_form = 'sij,bsi->bsj'
        else:
            piece = lax.dynamic_slice_in_dim(vectors, (grid_column * COLS_DEV).astype(jnp.int32), COLS_DEV, 1)
            in_index, out_index, out_blocks = (cols_here, rows_here, RB_DEV)
            einsum_form = 'sij,bsj->bsi'
        blocks = piece.reshape(batch, -1, TILE).astype(jnp.float32)
        picked = jnp.take(blocks, in_index, axis=1)
        products = jnp.einsum(einsum_form, tiles_here.astype(jnp.float32), picked, precision=lax.Precision.HIGHEST)
        live_slots = (jnp.arange(TILES_DEV, dtype=jnp.int32) < count_here).astype(jnp.float32)
        products = products * live_slots[None, :, None]
        selector = (out_index[:, None] == jnp.arange(out_blocks, dtype=jnp.int32)[None, :]).astype(jnp.float32)
        summed = jnp.einsum('sn,bsi->bni', selector, products, precision=lax.Precision.HIGHEST)
        return summed.reshape(batch, out_blocks * TILE)
    terms = lax.map(device_term, (stacked, rows_flat, cols_flat, counts, jnp.arange(devices, dtype=jnp.int32)))
    if transpose:
        summed = terms.reshape(N_ROW, N_COL, batch, COLS_DEV).sum(axis=0)
        return jnp.transpose(summed, (1, 0, 2)).reshape(batch, NCOL)
    summed = terms.reshape(N_ROW, N_COL, batch, ROWS_DEV).sum(axis=1)
    return jnp.transpose(summed, (1, 0, 2)).reshape(batch, NROW)

def reference(tile_data, tile_row_block, tile_column_block, tile_count, saved_primal, saved_dual, primal_mask, dual_mask, cost_vector, demand, upper_bound, step_sizes, primal_cotangent, dual_cotangent):
    tau = step_sizes[0]
    sigma = step_sizes[1]
    grid = (tile_data, tile_row_block, tile_column_block, tile_count)
    masks_x = primal_mask.astype(jnp.float32)
    masks_y = dual_mask.astype(jnp.float32)
    reduced = cost_vector[None, :] - apply_tiles(*grid, saved_dual.astype(jnp.bfloat16), True)
    half = jnp.clip(saved_primal - tau * reduced, 0.0, upper_bound[None, :])
    extrapolated = (2.0 * half - saved_primal).astype(jnp.bfloat16)
    residual = demand[None, :] - apply_tiles(*grid, extrapolated, False)
    adjoint_x = primal_cotangent
    adjoint_y = dual_cotangent
    anchor_x = jnp.zeros_like(adjoint_x)
    anchor_y = jnp.zeros_like(adjoint_y)
    tau_sum = jnp.zeros((), jnp.float32)
    sigma_sum = jnp.zeros((), jnp.float32)
    for step in reversed(range(ITERS)):
        weight = (step + 1.0) / (step + 2.0)
        anchor_x = anchor_x + (1.0 - weight) * adjoint_x
        anchor_y = anchor_y + (1.0 - weight) * adjoint_y
        dual_term = masks_y[step] * weight * adjoint_y
        sigma_sum = sigma_sum + jnp.sum(dual_term * residual[step])
        back = apply_tiles(*grid, dual_term.astype(jnp.bfloat16)[None, :], True)[0]
        primal_term = masks_x[step] * (weight * adjoint_x - 2.0 * sigma * back)
        tau_sum = tau_sum + jnp.sum(-primal_term * reduced[step])
        adjoint_x = primal_term + sigma * back
        image = apply_tiles(*grid, primal_term.astype(jnp.bfloat16)[None, :], False)[0]
        adjoint_y = dual_term + tau * image
    gradients = jnp.stack([tau_sum / math.sqrt(NCOL), sigma_sum / math.sqrt(NROW)])
    return (adjoint_x + anchor_x, adjoint_y + anchor_y, gradients)
```

```python
import functools
import math

import jax
import jax.numpy as jnp
from jax import lax
from jax.experimental import pallas as pl
from jax.experimental.pallas import tpu as pltpu
from jax.sharding import PartitionSpec as P

F32 = jnp.float32
BF16 = jnp.bfloat16
LANES = 128
NN = (((1,), (0,)), ((), ()))
NT = (((1,), (1,)), ((), ()))


def ring_offsets(n):
    return sorted(range(1, n), key=lambda r: -min(r, n - r))


def kernel(
    dims,
    tiles_hbm,
    rb_hbm,
    cb_hbm,
    count_hbm,
    primal_hbm,
    dual_hbm,
    pmask_hbm,
    dmask_hbm,
    cost_hbm,
    demand_hbm,
    upper_hbm,
    steps_hbm,
    pcot_hbm,
    dcot_hbm,
    padj_hbm,
    dadj_hbm,
    grad_hbm,
    tiles,
    rb_s,
    cb_s,
    count_s,
    steps_s,
    primal_in,
    dual_in,
    pmask_in,
    dmask_in,
    cost,
    demand,
    upper,
    pcot,
    dcot,
    primal,
    pmask,
    dmask,
    lhs,
    hi_rows,
    lo_rows,
    p_rows,
    z_send,
    z_recv,
    z3_send,
    z3_recv,
    hilo,
    p_all,
    x_all,
    c_lin,
    c_send,
    c_recv,
    d_all,
    out_all,
    dadj,
    sz_all,
    sc_all,
    grad,
    in_sem,
    send_sem,
    recv_sem,
):
    n_row, n_col, iters, slots = dims
    me_r = lax.axis_index("row")
    me_c = lax.axis_index("col")
    blocks = 64
    width = tiles.shape[-1]

    def fetch(i, src, dst):
        copy = pltpu.make_async_copy(src, dst, in_sem.at[i])
        copy.start()
        return copy

    z_lanes = primal_in.shape[1]
    small = [
        fetch(0, rb_hbm, rb_s),
        fetch(1, cb_hbm, cb_s),
        fetch(2, count_hbm, count_s),
        fetch(3, steps_hbm, steps_s),
        fetch(4, dmask_hbm, dmask_in),
        fetch(5, dcot_hbm, dcot),
    ]
    tile_copy = fetch(6, tiles_hbm, tiles)
    z_at = pl.ds(pl.multiple_of(me_r * z_lanes, LANES), z_lanes)
    rest = [
        fetch(7, dual_hbm, dual_in),
        fetch(8, primal_hbm.at[:, z_at], primal_in),
        fetch(9, pmask_hbm.at[:, z_at], pmask_in),
        fetch(10, cost_hbm.at[me_r], cost),
        fetch(11, upper_hbm.at[me_r], upper),
        fetch(12, pcot_hbm.at[me_r], pcot),
        fetch(13, demand_hbm.at[me_c], demand),
    ]

    z_peers = [(r, lax.rem(me_r + r, n_row)) for r in ring_offsets(n_row)]
    c_peers = [(r, lax.rem(me_c + r, n_col)) for r in range(1, n_col)]
    barrier = pltpu.get_barrier_semaphore()
    for _, r in z_peers:
        pl.semaphore_signal(barrier, inc=1, device_id={"row": r})
    for _, c in c_peers:
        pl.semaphore_signal(barrier, inc=1, device_id={"col": c})

    def send(sem, src, dst, peer):
        pltpu.make_async_remote_copy(
            src_ref=src,
            dst_ref=dst,
            send_sem=send_sem.at[sem],
            recv_sem=recv_sem.at[sem],
            device_id=peer,
            device_id_type=pl.DeviceIdType.MESH,
        ).start()

    def arrive(sem, ref):
        pltpu.make_async_copy(ref, ref, recv_sem.at[sem]).wait()

    def left(sem, ref):
        pltpu.make_async_copy(ref, ref, send_sem.at[sem]).wait()

    iota = lax.broadcasted_iota(jnp.int32, (blocks, LANES), 0)

    def spread(s, index_ref, halves):
        keep = iota == index_ref[0, s] + blocks * jnp.maximum(s + 1 - count_s[0, 0], 0)
        return [
            jnp.where(keep, jnp.broadcast_to(h, (blocks, LANES)), 0.0).astype(BF16) for h in halves
        ]

    def apply_transpose(vectors, pick):
        for s in range(slots):
            for v, halves in enumerate(pick(s)):
                for h, value in enumerate(spread(s, cb_s, halves)):
                    lhs[
                        v * blocks : (v + 1) * blocks,
                        s * width + h * LANES : s * width + (h + 1) * LANES,
                    ] = value
        return lax.dot_general(
            lhs[: vectors * blocks, :],
            tiles[...].reshape(slots * width, width),
            NN,
            preferred_element_type=F32,
        )

    def apply_forward():
        acc = jnp.zeros((blocks, width), F32)
        for s in range(slots):
            c = cb_s[0, s]
            b = lax.div(c, 8)
            i = 2 * lax.rem(c, 8)
            halves = [p_rows[b, pl.ds(i, 1), :], p_rows[b, pl.ds(i + 1, 1), :]]
            row = jnp.concatenate(spread(s, rb_s, halves), axis=1)
            acc = acc + lax.dot_general(row, tiles[s], NT, preferred_element_type=F32)
        return acc

    def store_z(dst, value):
        for j in range(n_row):
            for h in range(2):
                dst[j, pl.ds(h, 8, stride=2), :] = value[
                    8 * j : 8 * j + 8, h * LANES : (h + 1) * LANES
                ]

    for copy in small:
        copy.wait()
    tau = steps_s[0, 0]
    sigma = steps_s[0, 1]
    weights = [(k + 1.0) / (k + 2.0) for k in range(iters)]
    last = iters - 1

    def pick_start(s):
        r = rb_s[0, s]
        a = lax.div(r, 2)
        b = 2 * lax.rem(r, 2)
        his, los = [], []
        for h in range(2):
            mask = dmask_in[pl.ds(last, 1), pl.ds((2 * r + h) * LANES, LANES)]
            d = mask.astype(F32) * weights[last] * dcot[a, pl.ds(b + h, 1), :]
            hi = d.astype(BF16).astype(F32)
            his.append(hi)
            los.append(d - hi)
        return [his, los]

    def pick_d(s):
        r = rb_s[0, s]
        a = lax.div(r, 2)
        b = 2 * lax.rem(r, 2)
        return [
            [ref[a, pl.ds(b, 1), :], ref[a, pl.ds(b + 1, 1), :]] for ref in (hi_rows, lo_rows)
        ]

    def pick_dual(s):
        r = rb_s[0, s]
        return [
            [dual_in[pl.ds(k, 1), pl.ds((2 * r + h) * LANES, LANES)] for h in range(2)]
            for k in range(iters)
        ]

    def phase(k, which):
        return 4 * k + which

    Z3, XG, OUT, SZ, SC = (4 * iters + i for i in range(5))

    tile_copy.wait()

    tau_local = jnp.zeros((), F32)
    sigma_local = jnp.zeros((), F32)
    anchor_x = anchor_y = None
    ax = ay = d = None

    for k in reversed(range(iters)):
        weight = weights[k]
        if k == last:
            both = apply_transpose(2, pick_start)
        else:
            got = d_all[k]
            hi = got.astype(BF16).astype(F32)
            hi_rows[...] = hi
            lo_rows[...] = got - hi
            both = apply_transpose(2, pick_d)
        store_z(z_send.at[k], both[:blocks])
        if k == last:
            pl.semaphore_wait(barrier, len(z_peers) + len(c_peers))
        for r, peer in z_peers:
            send(phase(k, 0), z_send.at[k, peer], z_recv.at[k, r - 1], {"row": peer})
        store_z(hilo.at[k], both[:blocks] + both[blocks:])
        if k == last:
            for copy in rest:
                copy.wait()
            duals = apply_transpose(iters, pick_dual)
            for i in range(iters):
                for j in range(n_row):
                    for h in range(2):
                        z3_send[j, i, pl.ds(h, 8, stride=2), :] = duals[
                            i * blocks + 8 * j : i * blocks + 8 * j + 8,
                            h * LANES : (h + 1) * LANES,
                        ]
            for i in range(iters):
                for q in range(16):
                    cut = slice(q * LANES, (q + 1) * LANES)
                    primal[i, q : q + 1, :] = primal_in[i : i + 1, cut]
                    pmask[i, q : q + 1, :] = pmask_in[i : i + 1, cut].astype(F32)
                for q in range(4):
                    at = pl.multiple_of(me_c * (4 * LANES) + q * LANES, LANES)
                    dmask[i, q : q + 1, :] = dmask_in[i : i + 1, pl.ds(at, LANES)].astype(F32)
            ax = pcot[...]
            ay = dcot[me_c]
            anchor_x = (1.0 - weight) * ax
            anchor_y = (1.0 - weight) * ay
            d = dmask[k] * weight * ay
        else:
            if k == last - 1:
                arrive(XG, x_all.at[pl.ds(0, n_row - 1)])
                part = hilo[last] * x_all[:, last].astype(F32)
                sigma_local = sigma_local - jnp.sum(part)
            part = hilo[k] * x_all[:, k].astype(F32)
            sigma_local = sigma_local - jnp.sum(part)
        sigma_local = sigma_local + jnp.sum(d * demand[...])
        arrive(phase(k, 0), z_recv.at[k])
        back = z_send[k, me_r]
        for r in range(n_row - 1):
            back = back + z_recv[k, r]
        if k != last:
            anchor_x = anchor_x + (1.0 - weight) * ax
        p = pmask[k] * (weight * ax - (2.0 * sigma) * back)
        p_all[k, me_r] = p.astype(BF16)
        for _, peer in z_peers:
            send(phase(k, 1), p_all.at[k, me_r], p_all.at[k, me_r], {"row": peer})
        ax = p + sigma * back
        if k == 0:
            out_all[me_r] = ax + anchor_x
            for _, peer in z_peers:
                send(OUT, out_all.at[me_r], out_all.at[me_r], {"row": peer})
        if k == last:
            p_last = p
        else:
            tau_local = tau_local - jnp.sum(p * primal[k])
        if k == 0:
            lane = lax.broadcasted_iota(jnp.int32, (1, LANES), 1)
            sz_all[me_r] = jnp.where(lane == 0, tau_local, jnp.where(lane == 1, sigma_local, 0.0))
            for _, peer in z_peers:
                send(SZ, sz_all.at[me_r], sz_all.at[me_r], {"row": peer})
        arrive(phase(k, 1), p_all.at[k, pl.ds(0, n_row - 1)])
        if k == last:
            for r, peer in z_peers:
                send(Z3, z3_send.at[peer], z3_recv.at[r - 1], {"row": peer})
        p_rows[...] = p_all[k].astype(F32)
        image = apply_forward()
        c_lin[pl.ds(0, blocks, stride=2), :] = image[:, :LANES]
        c_lin[pl.ds(1, blocks, stride=2), :] = image[:, LANES:]
        c_send[k] = c_lin[...].reshape(n_col, 4, LANES)
        for r, peer in c_peers:
            send(phase(k, 2), c_send.at[k, peer], c_recv.at[k, r - 1], {"col": peer})
        if k == 0:
            arrive(SZ, sz_all.at[pl.ds(0, n_row - 1)])
            total = sz_all[0]
            for r in range(1, n_row):
                total = total + sz_all[r]
            sc_all[me_c] = total
            for _, peer in c_peers:
                send(SC, sc_all.at[me_c], sc_all.at[me_c], {"col": peer})
            arrive(OUT, out_all.at[pl.ds(0, n_row - 1)])
            padj_copy = pltpu.make_async_copy(out_all, padj_hbm, in_sem.at[0])
            padj_copy.start()
        arrive(phase(k, 2), c_recv.at[k])
        rows = c_send[k, me_c]
        for r in range(n_col - 1):
            rows = rows + c_recv[k, r]
        ay = d + tau * rows
        if k > 0:
            weight = weights[k - 1]
            anchor_y = anchor_y + (1.0 - weight) * ay
            d = dmask[k - 1] * weight * ay
            d_all[k - 1, me_c] = d
            for _, peer in c_peers:
                here = d_all.at[k - 1, me_c]
                send(phase(k - 1, 3), here, here, {"col": peer})
            if k == last:
                arrive(Z3, z3_recv)
                for i in range(iters):
                    column = z3_send[me_r, i]
                    for r in range(n_row - 1):
                        column = column + z3_recv[r, i]
                    reduced = cost[...] - column
                    saved = primal[i]
                    half = jnp.minimum(jnp.maximum(saved - tau * reduced, 0.0), upper[...])
                    x_all[me_r, i] = (2.0 * half - saved).astype(BF16)
                    primal[i] = reduced
                for _, peer in z_peers:
                    send(XG, x_all.at[me_r], x_all.at[me_r], {"row": peer})
                tau_local = tau_local - jnp.sum(p_last * primal[last])
            arrive(phase(k - 1, 3), d_all.at[k - 1, pl.ds(0, n_col - 1)])

    dadj[...] = ay + anchor_y
    dadj_copy = pltpu.make_async_copy(dadj, dadj_hbm, in_sem.at[1])
    dadj_copy.start()
    arrive(SC, sc_all.at[pl.ds(0, n_col - 1)])
    total = sc_all[0]
    for c in range(1, n_col):
        total = total + sc_all[c]
    lane = lax.broadcasted_iota(jnp.int32, (1, LANES), 1)
    columns = float(n_col * blocks * width)
    lines = float(n_row * blocks * width)
    grad[...] = total * jnp.where(lane == 0, 1.0 / math.sqrt(columns), 1.0 / math.sqrt(lines))
    grad_copy = pltpu.make_async_copy(grad, grad_hbm, in_sem.at[2])
    grad_copy.start()

    for k in range(iters):
        left(phase(k, 0), z_recv.at[k])
        left(phase(k, 1), p_all.at[k, pl.ds(0, n_row - 1)])
        left(phase(k, 2), c_recv.at[k])
        if k < last:
            left(phase(k, 3), d_all.at[k, pl.ds(0, n_col - 1)])
    left(Z3, z3_recv)
    left(XG, x_all.at[pl.ds(0, n_row - 1)])
    left(OUT, out_all.at[pl.ds(0, n_row - 1)])
    left(SZ, sz_all.at[pl.ds(0, n_row - 1)])
    left(SC, sc_all.at[pl.ds(0, n_col - 1)])
    padj_copy.wait()
    dadj_copy.wait()
    grad_copy.wait()


def local(
    tile_data,
    tile_row_block,
    tile_column_block,
    tile_count,
    saved_primal,
    saved_dual,
    primal_mask,
    dual_mask,
    cost_vector,
    demand,
    upper_bound,
    step_sizes,
    primal_cotangent,
    dual_cotangent,
):
    n_row = lax.axis_size("row")
    n_col = lax.axis_size("col")
    slots, width = tile_data.shape[2], tile_data.shape[-1]
    iters = saved_primal.shape[0]
    rows = saved_dual.shape[1]
    columns = saved_primal.shape[1]
    z_shape = (n_row, columns // n_row // LANES, LANES)
    c_shape = (n_col, rows // n_col // LANES, LANES)
    zq, cq = z_shape[1], c_shape[1]
    blocks = rows // width
    any_spec = pl.BlockSpec(memory_space=pl.ANY)
    phases = 4 * iters + 5
    outs = pl.pallas_call(
        functools.partial(kernel, (n_row, n_col, iters, slots)),
        out_shape=(
            jax.ShapeDtypeStruct(z_shape, F32),
            jax.ShapeDtypeStruct(c_shape[1:], F32),
            jax.ShapeDtypeStruct((1, LANES), F32),
        ),
        in_specs=[any_spec] * 14,
        out_specs=(any_spec,) * 3,
        scratch_shapes=[
            pltpu.VMEM((slots, width, width), BF16),
            pltpu.SMEM((1, slots), jnp.int32),
            pltpu.SMEM((1, slots), jnp.int32),
            pltpu.SMEM((1, 1), jnp.int32),
            pltpu.SMEM((1, 2), F32),
            pltpu.VMEM((iters, columns // n_row), F32),
            pltpu.VMEM((iters, rows), F32),
            pltpu.VMEM((iters, columns // n_row), jnp.int32),
            pltpu.VMEM((iters, rows), jnp.int32),
            pltpu.VMEM(z_shape[1:], F32),
            pltpu.VMEM(c_shape[1:], F32),
            pltpu.VMEM(z_shape[1:], F32),
            pltpu.VMEM(z_shape[1:], F32),
            pltpu.VMEM(c_shape, F32),
            pltpu.VMEM((iters, zq, LANES), F32),
            pltpu.VMEM((iters, zq, LANES), F32),
            pltpu.VMEM((iters, cq, LANES), F32),
            pltpu.VMEM((max(2, iters) * blocks, slots * width), BF16),
            pltpu.VMEM(c_shape, F32),
            pltpu.VMEM(c_shape, F32),
            pltpu.VMEM(z_shape, F32),
            pltpu.VMEM((iters,) + z_shape, F32),
            pltpu.VMEM((iters, n_row - 1, zq, LANES), F32),
            pltpu.VMEM((n_row, iters, zq, LANES), F32),
            pltpu.VMEM((n_row - 1, iters, zq, LANES), F32),
            pltpu.VMEM((iters,) + z_shape, F32),
            pltpu.VMEM((iters,) + z_shape, BF16),
            pltpu.VMEM((n_row, iters, zq, LANES), BF16),
            pltpu.VMEM((rows // LANES, LANES), F32),
            pltpu.VMEM((iters,) + c_shape, F32),
            pltpu.VMEM((iters, n_col - 1, cq, LANES), F32),
            pltpu.VMEM((iters - 1,) + c_shape, F32),
            pltpu.VMEM(z_shape, F32),
            pltpu.VMEM(c_shape[1:], F32),
            pltpu.VMEM((n_row, 1, LANES), F32),
            pltpu.VMEM((n_col, 1, LANES), F32),
            pltpu.VMEM((1, LANES), F32),
            pltpu.SemaphoreType.DMA((14,)),
            pltpu.SemaphoreType.DMA((phases,)),
            pltpu.SemaphoreType.DMA((phases,)),
        ],
        compiler_params=pltpu.CompilerParams(
            collective_id=0, has_side_effects=True, vmem_limit_bytes=40 << 20
        ),
        name="primal_dual_adjoint",
    )(
        tile_data.reshape(slots, width, width),
        tile_row_block.reshape(1, slots),
        tile_column_block.reshape(1, slots),
        tile_count.reshape(1, 1),
        saved_primal,
        saved_dual,
        primal_mask,
        dual_mask,
        cost_vector.reshape(z_shape),
        demand.reshape(c_shape),
        upper_bound.reshape(z_shape),
        step_sizes.reshape(1, 2),
        primal_cotangent.reshape(z_shape),
        dual_cotangent.reshape(c_shape),
    )
    return (outs[0].reshape(columns), outs[1].reshape(rows // n_col), outs[2][0, :2])


def solution(mesh):
    placed = (
        P("row", "col", None, None, None),
        P("row", "col", None),
        P("row", "col", None),
        P("row", "col"),
        P(None, "col"),
        P(None, "row"),
        P(None, "col"),
        P(None, "row"),
        P("col"),
        P("row"),
        P("col"),
        P(),
        P("col"),
        P("row"),
    )
    return jax.shard_map(
        local,
        mesh=mesh,
        in_specs=placed,
        out_specs=(P("col"), P(("row", "col")), P()),
        check_vma=False,
    )
```

```python
import functools
import math

import jax
import jax.numpy as jnp
from jax import lax
from jax.experimental import pallas as pl
from jax.experimental.pallas import tpu as pltpu
from jax.sharding import PartitionSpec as P

F32 = jnp.float32
BF16 = jnp.bfloat16
LANES = 128
NN = (((1,), (0,)), ((), ()))
NT = (((1,), (1,)), ((), ()))


def ring_offsets(n):
    return sorted(range(1, n), key=lambda r: -min(r, n - r))


def kernel(
    dims,
    tiles_hbm,
    rb_hbm,
    cb_hbm,
    count_hbm,
    primal_hbm,
    dual_hbm,
    pmask_hbm,
    dmask_hbm,
    cost_hbm,
    demand_hbm,
    upper_hbm,
    steps_hbm,
    pcot_hbm,
    dcot_hbm,
    padj_hbm,
    dadj_hbm,
    grad_hbm,
    tiles,
    rb_s,
    cb_s,
    count_s,
    steps_s,
    primal_in,
    dual_in,
    pmask_in,
    dmask_in,
    cost,
    demand,
    upper,
    pcot,
    dcot,
    primal,
    pmask,
    dmask,
    lhs,
    hi_rows,
    lo_rows,
    p_rows,
    z_send,
    z_recv,
    z3_send,
    z3_recv,
    hilo,
    p_all,
    x_all,
    c_lin,
    c_send,
    c_recv,
    d_all,
    out_all,
    dadj,
    sz_all,
    sc_all,
    grad,
    in_sem,
    send_sem,
    recv_sem,
):
    n_row, n_col, iters, slots = dims
    me_r = lax.axis_index("row")
    me_c = lax.axis_index("col")
    blocks = 64
    width = tiles.shape[-1]

    def fetch(i, src, dst):
        copy = pltpu.make_async_copy(src, dst, in_sem.at[i])
        copy.start()
        return copy

    z_lanes = primal_in.shape[1]
    small = [
        fetch(0, rb_hbm, rb_s),
        fetch(1, cb_hbm, cb_s),
        fetch(2, count_hbm, count_s),
        fetch(3, steps_hbm, steps_s),
        fetch(4, dmask_hbm, dmask_in),
        fetch(5, dcot_hbm, dcot),
    ]
    tile_copy = fetch(6, tiles_hbm, tiles)
    z_at = pl.ds(pl.multiple_of(me_r * z_lanes, LANES), z_lanes)
    rest = [
        fetch(7, dual_hbm, dual_in),
        fetch(8, primal_hbm.at[:, z_at], primal_in),
        fetch(9, pmask_hbm.at[:, z_at], pmask_in),
        fetch(10, cost_hbm.at[me_r], cost),
        fetch(11, upper_hbm.at[me_r], upper),
        fetch(12, pcot_hbm.at[me_r], pcot),
        fetch(13, demand_hbm.at[me_c], demand),
    ]

    z_peers = [(r, lax.rem(me_r + r, n_row)) for r in ring_offsets(n_row)]
    c_peers = [(r, lax.rem(me_c + r, n_col)) for r in range(1, n_col)]
    barrier = pltpu.get_barrier_semaphore()
    for _, r in z_peers:
        pl.semaphore_signal(barrier, inc=1, device_id={"row": r})
    for _, c in c_peers:
        pl.semaphore_signal(barrier, inc=1, device_id={"col": c})

    def send(sem, src, dst, peer):
        pltpu.make_async_remote_copy(
            src_ref=src,
            dst_ref=dst,
            send_sem=send_sem.at[sem],
            recv_sem=recv_sem.at[sem],
            device_id=peer,
            device_id_type=pl.DeviceIdType.MESH,
        ).start()

    def arrive(sem, ref):
        pltpu.make_async_copy(ref, ref, recv_sem.at[sem]).wait()

    def left(sem, ref):
        pltpu.make_async_copy(ref, ref, send_sem.at[sem]).wait()

    iota = lax.broadcasted_iota(jnp.int32, (blocks, LANES), 0)

    def spread(s, index_ref, halves):
        keep = iota == index_ref[0, s] + blocks * jnp.maximum(s + 1 - count_s[0], 0)
        return [
            jnp.where(keep, jnp.broadcast_to(h, (blocks, LANES)), 0.0).astype(BF16) for h in halves
        ]

    def apply_transpose(vectors, pick):
        for s in range(slots):
            for v, halves in enumerate(pick(s)):
                for h, value in enumerate(spread(s, cb_s, halves)):
                    lhs[
                        v * blocks : (v + 1) * blocks,
                        s * width + h * LANES : s * width + (h + 1) * LANES,
                    ] = value
        return lax.dot_general(
            lhs[: vectors * blocks, :],
            tiles[...].reshape(slots * width, width),
            NN,
            preferred_element_type=F32,
        )

    def apply_forward():
        acc = jnp.zeros((blocks, width), F32)
        for s in range(slots):
            c = cb_s[0, s]
            b = lax.div(c, 8)
            i = 2 * lax.rem(c, 8)
            halves = [p_rows[b, pl.ds(i, 1), :], p_rows[b, pl.ds(i + 1, 1), :]]
            row = jnp.concatenate(spread(s, rb_s, halves), axis=1)
            acc = acc + lax.dot_general(row, tiles[s], NT, preferred_element_type=F32)
        return acc

    def store_z(dst, value):
        for j in range(n_row):
            for h in range(2):
                dst[j, pl.ds(h, 8, stride=2), :] = value[
                    8 * j : 8 * j + 8, h * LANES : (h + 1) * LANES
                ]

    for copy in small:
        copy.wait()
    tau = steps_s[0, 0]
    sigma = steps_s[0, 1]
    weights = [(k + 1.0) / (k + 2.0) for k in range(iters)]
    last = iters - 1

    def pick_start(s):
        r = rb_s[0, s]
        a = lax.div(r, 2)
        b = 2 * lax.rem(r, 2)
        his, los = [], []
        for h in range(2):
            mask = dmask_in[pl.ds(last, 1), pl.ds((2 * r + h) * LANES, LANES)]
            d = mask.astype(F32) * weights[last] * dcot[a, pl.ds(b + h, 1), :]
            hi = d.astype(BF16).astype(F32)
            his.append(hi)
            los.append(d - hi)
        return [his, los]

    def pick_d(s):
        r = rb_s[0, s]
        a = lax.div(r, 2)
        b = 2 * lax.rem(r, 2)
        return [
            [ref[a, pl.ds(b, 1), :], ref[a, pl.ds(b + 1, 1), :]] for ref in (hi_rows, lo_rows)
        ]

    def pick_dual(s):
        r = rb_s[0, s]
        return [
            [dual_in[pl.ds(k, 1), pl.ds((2 * r + h) * LANES, LANES)] for h in range(2)]
            for k in range(iters)
        ]

    def phase(k, which):
        return 4 * k + which

    Z3, XG, OUT, SZ, SC = (4 * iters + i for i in range(5))

    tile_copy.wait()

    tau_local = jnp.zeros((), F32)
    sigma_local = jnp.zeros((), F32)
    anchor_x = anchor_y = None
    ax = ay = d = None

    for k in reversed(range(iters)):
        weight = weights[k]
        if k == last:
            both = apply_transpose(2, pick_start)
        else:
            got = d_all[k]
            hi = got.astype(BF16).astype(F32)
            hi_rows[...] = hi
            lo_rows[...] = got - hi
            both = apply_transpose(2, pick_d)
        store_z(z_send.at[k], both[:blocks])
        if k == last:
            pl.semaphore_wait(barrier, len(z_peers) + len(c_peers))
        for r, peer in z_peers:
            send(phase(k, 0), z_send.at[k, peer], z_recv.at[k, r - 1], {"row": peer})
        store_z(hilo.at[k], both[:blocks] + both[blocks:])
        if k == last:
            for copy in rest:
                copy.wait()
            duals = apply_transpose(iters, pick_dual)
            for i in range(iters):
                for j in range(n_row):
                    for h in range(2):
                        z3_send[j, i, pl.ds(h, 8, stride=2), :] = duals[
                            i * blocks + 8 * j : i * blocks + 8 * j + 8,
                            h * LANES : (h + 1) * LANES,
                        ]
            for i in range(iters):
                for q in range(16):
                    cut = slice(q * LANES, (q + 1) * LANES)
                    primal[i, q : q + 1, :] = primal_in[i : i + 1, cut]
                    pmask[i, q : q + 1, :] = pmask_in[i : i + 1, cut].astype(F32)
                for q in range(4):
                    at = pl.multiple_of(me_c * (4 * LANES) + q * LANES, LANES)
                    dmask[i, q : q + 1, :] = dmask_in[i : i + 1, pl.ds(at, LANES)].astype(F32)
            ax = pcot[...]
            ay = dcot[me_c]
            anchor_x = (1.0 - weight) * ax
            anchor_y = (1.0 - weight) * ay
            d = dmask[k] * weight * ay
        else:
            if k == last - 1:
                arrive(XG, x_all.at[pl.ds(0, n_row - 1)])
                part = hilo[last] * x_all[:, last].astype(F32)
                sigma_local = sigma_local - jnp.sum(part)
            part = hilo[k] * x_all[:, k].astype(F32)
            sigma_local = sigma_local - jnp.sum(part)
        sigma_local = sigma_local + jnp.sum(d * demand[...])
        arrive(phase(k, 0), z_recv.at[k])
        back = z_send[k, me_r]
        for r in range(n_row - 1):
            back = back + z_recv[k, r]
        if k != last:
            anchor_x = anchor_x + (1.0 - weight) * ax
        p = pmask[k] * (weight * ax - (2.0 * sigma) * back)
        p_all[k, me_r] = p.astype(BF16)
        for _, peer in z_peers:
            send(phase(k, 1), p_all.at[k, me_r], p_all.at[k, me_r], {"row": peer})
        ax = p + sigma * back
        if k == 0:
            out_all[me_r] = ax + anchor_x
            for _, peer in z_peers:
                send(OUT, out_all.at[me_r], out_all.at[me_r], {"row": peer})
        if k == last:
            p_last = p
        else:
            tau_local = tau_local - jnp.sum(p * primal[k])
        if k == 0:
            lane = lax.broadcasted_iota(jnp.int32, (1, LANES), 1)
            sz_all[me_r] = jnp.where(lane == 0, tau_local, jnp.where(lane == 1, sigma_local, 0.0))
            for _, peer in z_peers:
                send(SZ, sz_all.at[me_r], sz_all.at[me_r], {"row": peer})
        arrive(phase(k, 1), p_all.at[k, pl.ds(0, n_row - 1)])
        if k == last:
            for r, peer in z_peers:
                send(Z3, z3_send.at[peer], z3_recv.at[r - 1], {"row": peer})
        p_rows[...] = p_all[k].astype(F32)
        image = apply_forward()
        c_lin[pl.ds(0, blocks, stride=2), :] = image[:, :LANES]
        c_lin[pl.ds(1, blocks, stride=2), :] = image[:, LANES:]
        c_send[k] = c_lin[...].reshape(n_col, 4, LANES)
        for r, peer in c_peers:
            send(phase(k, 2), c_send.at[k, peer], c_recv.at[k, r - 1], {"col": peer})
        if k == 0:
            arrive(SZ, sz_all.at[pl.ds(0, n_row - 1)])
            total = sz_all[0]
            for r in range(1, n_row):
                total = total + sz_all[r]
            sc_all[me_c] = total
            for _, peer in c_peers:
                send(SC, sc_all.at[me_c], sc_all.at[me_c], {"col": peer})
            arrive(OUT, out_all.at[pl.ds(0, n_row - 1)])
            padj_copy = pltpu.make_async_copy(out_all, padj_hbm, in_sem.at[0])
            padj_copy.start()
        arrive(phase(k, 2), c_recv.at[k])
        rows = c_send[k, me_c]
        for r in range(n_col - 1):
            rows = rows + c_recv[k, r]
        ay = d + tau * rows
        if k > 0:
            weight = weights[k - 1]
            anchor_y = anchor_y + (1.0 - weight) * ay
            d = dmask[k - 1] * weight * ay
            d_all[k - 1, me_c] = d
            for _, peer in c_peers:
                here = d_all.at[k - 1, me_c]
                send(phase(k - 1, 3), here, here, {"col": peer})
            if k == last:
                arrive(Z3, z3_recv)
                for i in range(iters):
                    column = z3_send[me_r, i]
                    for r in range(n_row - 1):
                        column = column + z3_recv[r, i]
                    reduced = cost[...] - column
                    saved = primal[i]
                    half = jnp.minimum(jnp.maximum(saved - tau * reduced, 0.0), upper[...])
                    x_all[me_r, i] = (2.0 * half - saved).astype(BF16)
                    primal[i] = reduced
                for _, peer in z_peers:
                    send(XG, x_all.at[me_r], x_all.at[me_r], {"row": peer})
                tau_local = tau_local - jnp.sum(p_last * primal[last])
            arrive(phase(k - 1, 3), d_all.at[k - 1, pl.ds(0, n_col - 1)])

    dadj[...] = ay + anchor_y
    dadj_copy = pltpu.make_async_copy(dadj, dadj_hbm, in_sem.at[1])
    dadj_copy.start()
    arrive(SC, sc_all.at[pl.ds(0, n_col - 1)])
    total = sc_all[0]
    for c in range(1, n_col):
        total = total + sc_all[c]
    lane = lax.broadcasted_iota(jnp.int32, (1, LANES), 1)
    columns = float(n_col * blocks * width)
    lines = float(n_row * blocks * width)
    grad[...] = total * jnp.where(lane == 0, 1.0 / math.sqrt(columns), 1.0 / math.sqrt(lines))
    grad_copy = pltpu.make_async_copy(grad, grad_hbm, in_sem.at[2])
    grad_copy.start()

    for k in range(iters):
        left(phase(k, 0), z_recv.at[k])
        left(phase(k, 1), p_all.at[k, pl.ds(0, n_row - 1)])
        left(phase(k, 2), c_recv.at[k])
        if k < last:
            left(phase(k, 3), d_all.at[k, pl.ds(0, n_col - 1)])
    left(Z3, z3_recv)
    left(XG, x_all.at[pl.ds(0, n_row - 1)])
    left(OUT, out_all.at[pl.ds(0, n_row - 1)])
    left(SZ, sz_all.at[pl.ds(0, n_row - 1)])
    left(SC, sc_all.at[pl.ds(0, n_col - 1)])
    padj_copy.wait()
    dadj_copy.wait()
    grad_copy.wait()


def local(
    tile_data,
    tile_row_block,
    tile_column_block,
    tile_count,
    saved_primal,
    saved_dual,
    primal_mask,
    dual_mask,
    cost_vector,
    demand,
    upper_bound,
    step_sizes,
    primal_cotangent,
    dual_cotangent,
):
    n_row = lax.axis_size("row")
    n_col = lax.axis_size("col")
    slots, width = tile_data.shape[2], tile_data.shape[-1]
    iters = saved_primal.shape[0]
    rows = saved_dual.shape[1]
    columns = saved_primal.shape[1]
    z_shape = (n_row, columns // n_row // LANES, LANES)
    c_shape = (n_col, rows // n_col // LANES, LANES)
    zq, cq = z_shape[1], c_shape[1]
    blocks = rows // width
    any_spec = pl.BlockSpec(memory_space=pltpu.HBM)
    phases = 4 * iters + 5
    outs = pl.pallas_call(
        functools.partial(kernel, (n_row, n_col, iters, slots)),
        out_shape=(
            jax.ShapeDtypeStruct(z_shape, F32),
            jax.ShapeDtypeStruct(c_shape[1:], F32),
            jax.ShapeDtypeStruct((1, LANES), F32),
        ),
        in_specs=[any_spec] * 14,
        out_specs=(any_spec,) * 3,
        scratch_shapes=[
            pltpu.VMEM((slots, width, width), BF16),
            pltpu.SMEM((1, slots), jnp.int32),
            pltpu.SMEM((1, slots), jnp.int32),
            pltpu.SMEM((1,), jnp.int32),
            pltpu.SMEM((1, 2), F32),
            pltpu.VMEM((iters, columns // n_row), F32),
            pltpu.VMEM((iters, rows), F32),
            pltpu.VMEM((iters, columns // n_row), jnp.int32),
            pltpu.VMEM((iters, rows), jnp.int32),
            pltpu.VMEM(z_shape[1:], F32),
            pltpu.VMEM(c_shape[1:], F32),
            pltpu.VMEM(z_shape[1:], F32),
            pltpu.VMEM(z_shape[1:], F32),
            pltpu.VMEM(c_shape, F32),
            pltpu.VMEM((iters, zq, LANES), F32),
            pltpu.VMEM((iters, zq, LANES), F32),
            pltpu.VMEM((iters, cq, LANES), F32),
            pltpu.VMEM((max(2, iters) * blocks, slots * width), BF16),
            pltpu.VMEM(c_shape, F32),
            pltpu.VMEM(c_shape, F32),
            pltpu.VMEM(z_shape, F32),
            pltpu.VMEM((iters,) + z_shape, F32),
            pltpu.VMEM((iters, n_row - 1, zq, LANES), F32),
            pltpu.VMEM((n_row, iters, zq, LANES), F32),
            pltpu.VMEM((n_row - 1, iters, zq, LANES), F32),
            pltpu.VMEM((iters,) + z_shape, F32),
            pltpu.VMEM((iters,) + z_shape, BF16),
            pltpu.VMEM((n_row, iters, zq, LANES), BF16),
            pltpu.VMEM((rows // LANES, LANES), F32),
            pltpu.VMEM((iters,) + c_shape, F32),
            pltpu.VMEM((iters, n_col - 1, cq, LANES), F32),
            pltpu.VMEM((iters - 1,) + c_shape, F32),
            pltpu.VMEM(z_shape, F32),
            pltpu.VMEM(c_shape[1:], F32),
            pltpu.VMEM((n_row, 1, LANES), F32),
            pltpu.VMEM((n_col, 1, LANES), F32),
            pltpu.VMEM((1, LANES), F32),
            pltpu.SemaphoreType.DMA((14,)),
            pltpu.SemaphoreType.DMA((phases,)),
            pltpu.SemaphoreType.DMA((phases,)),
        ],
        compiler_params=pltpu.CompilerParams(
            collective_id=0, has_side_effects=True, vmem_limit_bytes=64 << 20
        ),
        name="primal_dual_adjoint",
    )(
        tile_data.reshape(slots, width, width),
        tile_row_block.reshape(1, slots),
        tile_column_block.reshape(1, slots),
        tile_count.reshape(1),
        saved_primal,
        saved_dual,
        primal_mask,
        dual_mask,
        cost_vector.reshape(z_shape),
        demand.reshape(c_shape),
        upper_bound.reshape(z_shape),
        step_sizes.reshape(1, 2),
        primal_cotangent.reshape(z_shape),
        dual_cotangent.reshape(c_shape),
    )
    return (outs[0].reshape(columns), outs[1].reshape(rows // n_col), outs[2][0, :2])


def solution(mesh):
    placed = (
        P("row", "col", None, None, None),
        P("row", "col", None),
        P("row", "col", None),
        P("row", "col"),
        P(None, "col"),
        P(None, "row"),
        P(None, "col"),
        P(None, "row"),
        P("col"),
        P("row"),
        P("col"),
        P(),
        P("col"),
        P("row"),
    )
    return jax.shard_map(
        local,
        mesh=mesh,
        in_specs=placed,
        out_specs=(P("col"), P(("row", "col")), P()),
        check_vma=False,
    )
```

```python
import functools
import math

import jax
import jax.numpy as jnp
from jax import lax
from jax.experimental import pallas as pl
from jax.experimental.pallas import tpu as pltpu
from jax.sharding import PartitionSpec as P

F32 = jnp.float32
BF16 = jnp.bfloat16
LANES = 128
NN = (((1,), (0,)), ((), ()))
NT = (((1,), (1,)), ((), ()))


def ring_offsets(n):
    return sorted(range(1, n), key=lambda r: -min(r, n - r))


def kernel(
    dims,
    tiles_hbm,
    rb_hbm,
    cb_hbm,
    count_hbm,
    primal_hbm,
    dual_hbm,
    pmask_hbm,
    dmask_hbm,
    cost_hbm,
    demand_hbm,
    upper_hbm,
    steps_hbm,
    pcot_hbm,
    dcot_hbm,
    padj_hbm,
    dadj_hbm,
    grad_hbm,
    tiles,
    turned,
    rb_s,
    cb_s,
    count_s,
    steps_s,
    primal_in,
    dual_in,
    pmask_in,
    dmask_in,
    cost,
    demand,
    upper,
    pcot,
    dcot,
    primal,
    pmask,
    dmask,
    lhs,
    picked,
    picked_mask,
    p_rows,
    z_lin,
    z_send,
    z_recv,
    z3_send,
    z3_recv,
    hilo,
    prod_all,
    ax_all,
    x_all,
    rm_all,
    idx_all,
    c_lin,
    c_send,
    c_recv,
    d_all,
    out_all,
    dadj,
    sz_all,
    sc_all,
    grad,
    in_sem,
    send_sem,
    recv_sem,
):
    n_row, n_col, iters, slots = dims
    me_r = lax.axis_index("row")
    me_c = lax.axis_index("col")
    blocks = 64
    width = tiles.shape[-1]
    group = 8

    def fetch(i, src, dst):
        copy = pltpu.make_async_copy(src, dst, in_sem.at[i])
        copy.start()
        return copy

    z_lanes = primal_in.shape[1]
    small = [
        fetch(0, rb_hbm, rb_s),
        fetch(1, cb_hbm, cb_s),
        fetch(2, count_hbm, count_s),
        fetch(3, steps_hbm, steps_s),
        fetch(4, dmask_hbm, dmask_in),
        fetch(5, dcot_hbm, dcot),
    ]
    tile_copies = [
        fetch(14 + g, tiles_hbm.at[pl.ds(g * group, group)], tiles.at[pl.ds(g * group, group)])
        for g in range(slots // group)
    ]
    z_at = pl.ds(pl.multiple_of(me_r * z_lanes, LANES), z_lanes)
    rest = [
        fetch(6, dual_hbm, dual_in),
        fetch(7, primal_hbm.at[:, z_at], primal_in),
        fetch(8, pmask_hbm, pmask_in),
        fetch(9, cost_hbm.at[me_r], cost),
        fetch(10, upper_hbm.at[me_r], upper),
        fetch(11, pcot_hbm, pcot),
        fetch(12, demand_hbm.at[me_c], demand),
    ]

    z_peers = [(r, lax.rem(me_r + r, n_row)) for r in ring_offsets(n_row)]
    c_peers = [(r, lax.rem(me_c + r, n_col)) for r in range(1, n_col)]
    barrier = pltpu.get_barrier_semaphore()
    for _, r in z_peers:
        pl.semaphore_signal(barrier, inc=1, device_id={"row": r})
    for _, c in c_peers:
        pl.semaphore_signal(barrier, inc=1, device_id={"col": c})

    def send(sem, src, dst, peer):
        pltpu.make_async_remote_copy(
            src_ref=src,
            dst_ref=dst,
            send_sem=send_sem.at[sem],
            recv_sem=recv_sem.at[sem],
            device_id=peer,
            device_id_type=pl.DeviceIdType.MESH,
        ).start()

    def gather_z(sem, here):
        for _, peer in z_peers:
            send(sem, here, here, {"row": peer})

    def gather_c(sem, here):
        for _, peer in c_peers:
            send(sem, here, here, {"col": peer})

    def arrive(sem, ref):
        pltpu.make_async_copy(ref, ref, recv_sem.at[sem]).wait()

    def left(sem, ref):
        pltpu.make_async_copy(ref, ref, send_sem.at[sem]).wait()

    def others(n):
        return pl.ds(0, n - 1)

    SCATTER, PROD, FOLD, DUAL, AX = range(5)

    def phase(k, which):
        return 5 * k + which

    Z3, XG, RM, OUT, SZ, SC, IDX = (5 * iters + i for i in range(7))

    for copy in small:
        copy.wait()
    tau = steps_s[0, 0]
    sigma = steps_s[0, 1]
    weights = [(k + 1.0) / (k + 2.0) for k in range(iters)]
    last = iters - 1

    iota = lax.broadcasted_iota(jnp.int32, (blocks, LANES), 0)
    iota8 = lax.broadcasted_iota(jnp.int32, (group, width), 0)

    def live_block(s, index_ref):
        return index_ref[0, s] + blocks * jnp.maximum(s + 1 - count_s[0], 0)

    def spread(s, index_ref, halves):
        keep = iota == live_block(s, index_ref)
        return [
            jnp.where(keep, jnp.broadcast_to(h, (blocks, LANES)), 0.0).astype(BF16) for h in halves
        ]

    def dot(a, b):
        return lax.dot_general(a, b, NN, preferred_element_type=F32)

    def slot_products(value, wait=None):
        hi = value.astype(BF16).astype(F32)
        lo = value - hi
        his, los = [], []
        for g in range(slots // group):
            if wait is not None:
                wait[g].wait()
            cut = slice(g * group, (g + 1) * group)
            rows = jnp.concatenate([hi[cut], lo[cut]], axis=0).astype(BF16)
            ph = jnp.zeros((group, width), F32)
            po = jnp.zeros((group, width), F32)
            for i in range(group):
                both = dot(rows, tiles[g * group + i])
                ph = jnp.where(iota8 == i, both[:group], ph)
                po = jnp.where(iota8 == i, both[group:], po)
            his.append(ph)
            los.append(po)
        return jnp.concatenate(his, axis=0), jnp.concatenate(los, axis=0)

    def scatter(hot, value):
        a = value.astype(BF16)
        r = value - a.astype(F32)
        b = r.astype(BF16)
        c = (r - b.astype(F32)).astype(BF16)
        return dot(hot, jnp.concatenate([a, b, c, jnp.zeros_like(a)], axis=0))

    def apply_duals():
        for s in range(slots):
            r = rb_s[0, s]
            for v in range(iters):
                halves = [dual_in[pl.ds(v, 1), pl.ds((2 * r + h) * LANES, LANES)] for h in range(2)]
                for h, value in enumerate(spread(s, cb_s, halves)):
                    lhs[
                        v * blocks : (v + 1) * blocks,
                        s * width + h * LANES : s * width + (h + 1) * LANES,
                    ] = value
        return dot(lhs[...], tiles[...].reshape(slots * width, width))

    def apply_forward():
        acc = jnp.zeros((blocks, width), F32)
        for s in range(slots):
            c = cb_s[0, s]
            b = lax.div(c, 8)
            i = 2 * lax.rem(c, 8)
            halves = [p_rows[b, pl.ds(i, 1), :], p_rows[b, pl.ds(i + 1, 1), :]]
            row = jnp.concatenate(spread(s, rb_s, halves), axis=1)
            acc = acc + dot(row, turned[s])
        return acc

    def store_z(dst, value):
        for j in range(n_row):
            for h in range(2):
                dst[j, pl.ds(h, 8, stride=2), :] = value[
                    8 * j : 8 * j + 8, h * LANES : (h + 1) * LANES
                ]

    for s in range(slots):
        r = rb_s[0, s]
        a = lax.div(r, 2)
        b = 2 * lax.rem(r, 2)
        for h in range(2):
            cut = slice(h * LANES, (h + 1) * LANES)
            picked[s : s + 1, cut] = dcot[a, pl.ds(b + h, 1), :]
            picked_mask[s : s + 1, cut] = dmask_in[pl.ds(last, 1), pl.ds((2 * r + h) * LANES, LANES)]
    start = picked_mask[...].astype(F32) * weights[last] * picked[...]

    tau_local = jnp.zeros((), F32)
    sigma_local = jnp.zeros((), F32)
    anchor_x = anchor_y = None
    ax = ay = d = None
    hot = hot_all = None

    for k in reversed(range(iters)):
        weight = weights[k]
        if k == last:
            ph, po = slot_products(start, tile_copies)
        else:
            for s in range(slots):
                r = rb_s[0, s]
                a = lax.div(r, 2)
                b = 2 * lax.rem(r, 2)
                for h in range(2):
                    cut = slice(h * LANES, (h + 1) * LANES)
                    picked[s : s + 1, cut] = d_all[k, a, pl.ds(b + h, 1), :]
            ph, po = slot_products(picked[...])
        prod_all[k, me_r] = ph.astype(BF16)
        if k == last:
            lane2 = lax.broadcasted_iota(jnp.int32, (1, 2 * LANES), 1)
            lane = lax.broadcasted_iota(jnp.int32, (1, LANES), 1)
            mine = jnp.full((1, 2 * LANES), -1, jnp.int32)
            own = jnp.full((1, LANES), -1, jnp.int32)
            for s in range(slots):
                block = live_block(s, cb_s)
                mine = jnp.where(lane2 == me_r * slots + s, block, mine)
                own = jnp.where(lax.rem(lane, slots) == s, block, own)
            idx_all[me_r] = mine.astype(F32)
            hot = jnp.where(iota == own, 1.0, 0.0).astype(BF16)
            pl.semaphore_wait(barrier, len(z_peers) + len(c_peers))
        gather_z(phase(k, PROD), prod_all.at[k, me_r])
        if k == last:
            gather_z(IDX, idx_all.at[me_r])
        store_z(z_send.at[k], scatter(hot, ph))
        for r, peer in z_peers:
            send(phase(k, SCATTER), z_send.at[k, peer], z_recv.at[k, r - 1], {"row": peer})
        store_z(hilo.at[k], scatter(hot, ph + po))
        if k == last:
            for copy in rest:
                copy.wait()
            duals = apply_duals()
            for i in range(iters):
                for j in range(n_row):
                    for h in range(2):
                        z3_send[j, i, pl.ds(h, 8, stride=2), :] = duals[
                            i * blocks + 8 * j : i * blocks + 8 * j + 8,
                            h * LANES : (h + 1) * LANES,
                        ]
            for i in range(iters):
                for j in range(n_row):
                    for q in range(16):
                        at = (16 * j + q) * LANES
                        pmask[i, j, q : q + 1, :] = pmask_in[i : i + 1, at : at + LANES]
                for q in range(16):
                    primal[i, q : q + 1, :] = primal_in[i : i + 1, q * LANES : (q + 1) * LANES]
                for q in range(4):
                    at = pl.multiple_of(me_c * (4 * LANES) + q * LANES, LANES)
                    dmask[i, q : q + 1, :] = dmask_in[i : i + 1, pl.ds(at, LANES)].astype(F32)
            for s in range(slots):
                turned[s] = tiles[s].T
            ax = pcot[me_r]
            ay = dcot[me_c]
            anchor_x = (1.0 - weight) * ax
            anchor_y = (1.0 - weight) * ay
            d = dmask[k] * weight * ay
        else:
            if k == last - 1:
                arrive(XG, x_all.at[others(n_row)])
                arrive(RM, rm_all.at[others(n_row)])
                sigma_local = sigma_local - jnp.sum(hilo[last] * x_all[:, last].astype(F32))
            sigma_local = sigma_local - jnp.sum(hilo[k] * x_all[:, k].astype(F32))
        sigma_local = sigma_local + jnp.sum(d * demand[...])
        if k == 0:
            held = pmask[0, me_r].astype(F32) * weight * ax * primal[0]
            tau_local = tau_local - jnp.sum(held) + (2.0 * sigma) * jnp.sum(z_send[0] * rm_all[...])
            lane = lax.broadcasted_iota(jnp.int32, (1, LANES), 1)
            sz_all[me_r] = jnp.where(lane == 0, tau_local, jnp.where(lane == 1, sigma_local, 0.0))
            gather_z(SZ, sz_all.at[me_r])
        if k == last:
            arrive(IDX, idx_all.at[others(n_row)])
            index = idx_all[0]
            for r in range(1, n_row):
                index = jnp.maximum(index, idx_all[r])
            rows = lax.broadcasted_iota(jnp.int32, (blocks, 2 * LANES), 0).astype(F32)
            hot_all = jnp.where(rows == index, 1.0, 0.0).astype(BF16)
            ax_full = pcot[...]
        else:
            arrive(phase(k + 1, AX), ax_all.at[k, others(n_row)])
            ax_full = ax_all[k]
        arrive(phase(k, PROD), prod_all.at[k, others(n_row)])
        store_z(z_lin, dot(hot_all, prod_all[k].reshape(n_row * slots, width)))
        p_full = pmask[k].astype(F32) * (weight * ax_full - (2.0 * sigma) * z_lin[...])
        p_rows[...] = p_full.astype(BF16).astype(F32)
        if k == last:
            for r, peer in z_peers:
                send(Z3, z3_send.at[peer], z3_recv.at[r - 1], {"row": peer})
        image = apply_forward()
        c_lin[pl.ds(0, blocks, stride=2), :] = image[:, :LANES]
        c_lin[pl.ds(1, blocks, stride=2), :] = image[:, LANES:]
        c_send[k] = c_lin[...].reshape(n_col, 4, LANES)
        for r, peer in c_peers:
            send(phase(k, FOLD), c_send.at[k, peer], c_recv.at[k, r - 1], {"col": peer})
        if k == 0:
            arrive(SZ, sz_all.at[others(n_row)])
            total = sz_all[0]
            for r in range(1, n_row):
                total = total + sz_all[r]
            sc_all[me_c] = total
            gather_c(SC, sc_all.at[me_c])
        arrive(phase(k, SCATTER), z_recv.at[k])
        back = z_send[k, me_r]
        for r in range(n_row - 1):
            back = back + z_recv[k, r]
        if k != last:
            anchor_x = anchor_x + (1.0 - weight) * ax
        p = pmask[k, me_r].astype(F32) * (weight * ax - (2.0 * sigma) * back)
        ax = p + sigma * back
        if k > 0:
            ax_all[k - 1, me_r] = ax
            gather_z(phase(k, AX), ax_all.at[k - 1, me_r])
        else:
            out_all[me_r] = ax + anchor_x
            gather_z(OUT, out_all.at[me_r])
        if k == last:
            p_last = p
        elif k > 0:
            tau_local = tau_local - jnp.sum(p * primal[k])
        arrive(phase(k, FOLD), c_recv.at[k])
        rows = c_send[k, me_c]
        for r in range(n_col - 1):
            rows = rows + c_recv[k, r]
        ay = d + tau * rows
        if k > 0:
            weight = weights[k - 1]
            anchor_y = anchor_y + (1.0 - weight) * ay
            d = dmask[k - 1] * weight * ay
            d_all[k - 1, me_c] = d
            gather_c(phase(k - 1, DUAL), d_all.at[k - 1, me_c])
            if k == last:
                arrive(Z3, z3_recv)
                for i in range(iters):
                    column = z3_send[me_r, i]
                    for r in range(n_row - 1):
                        column = column + z3_recv[r, i]
                    reduced = cost[...] - column
                    saved = primal[i]
                    half = jnp.minimum(jnp.maximum(saved - tau * reduced, 0.0), upper[...])
                    x_all[me_r, i] = (2.0 * half - saved).astype(BF16)
                    primal[i] = reduced
                rm_all[me_r] = pmask[0, me_r].astype(F32) * primal[0]
                gather_z(XG, x_all.at[me_r])
                gather_z(RM, rm_all.at[me_r])
                tau_local = tau_local - jnp.sum(p_last * primal[last])
            arrive(phase(k - 1, DUAL), d_all.at[k - 1, others(n_col)])

    dadj[...] = ay + anchor_y
    dadj_copy = pltpu.make_async_copy(dadj, dadj_hbm, in_sem.at[1])
    dadj_copy.start()
    arrive(OUT, out_all.at[others(n_row)])
    padj_copy = pltpu.make_async_copy(out_all, padj_hbm, in_sem.at[0])
    padj_copy.start()
    arrive(SC, sc_all.at[others(n_col)])
    total = sc_all[0]
    for c in range(1, n_col):
        total = total + sc_all[c]
    lane = lax.broadcasted_iota(jnp.int32, (1, LANES), 1)
    columns = float(n_col * blocks * width)
    lines = float(n_row * blocks * width)
    scaled = total * jnp.where(lane == 0, 1.0 / math.sqrt(columns), 1.0 / math.sqrt(lines))
    grad[...] = scaled[:, :2]
    grad_copy = pltpu.make_async_copy(grad, grad_hbm, in_sem.at[2])
    grad_copy.start()

    for k in range(iters):
        left(phase(k, SCATTER), z_recv.at[k])
        left(phase(k, PROD), prod_all.at[k, others(n_row)])
        left(phase(k, FOLD), c_recv.at[k])
        if k < last:
            left(phase(k, DUAL), d_all.at[k, others(n_col)])
        if k > 0:
            left(phase(k, AX), ax_all.at[k - 1, others(n_row)])
    left(Z3, z3_recv)
    left(XG, x_all.at[others(n_row)])
    left(RM, rm_all.at[others(n_row)])
    left(IDX, idx_all.at[others(n_row)])
    left(OUT, out_all.at[others(n_row)])
    left(SZ, sz_all.at[others(n_row)])
    left(SC, sc_all.at[others(n_col)])
    padj_copy.wait()
    dadj_copy.wait()
    grad_copy.wait()


def hand_over(padj_in, dadj_in, grad_in, padj, dadj, grad, sem):
    copies = [
        pltpu.make_async_copy(src, dst, sem.at[i])
        for i, (src, dst) in enumerate(((padj_in, padj), (dadj_in, dadj), (grad_in, grad)))
    ]
    for copy in copies:
        copy.start()
    for copy in copies:
        copy.wait()


def local(
    tile_data,
    tile_row_block,
    tile_column_block,
    tile_count,
    saved_primal,
    saved_dual,
    primal_mask,
    dual_mask,
    cost_vector,
    demand,
    upper_bound,
    step_sizes,
    primal_cotangent,
    dual_cotangent,
):
    n_row = lax.axis_size("row")
    n_col = lax.axis_size("col")
    slots, width = tile_data.shape[2], tile_data.shape[-1]
    iters = saved_primal.shape[0]
    rows = saved_dual.shape[1]
    columns = saved_primal.shape[1]
    z_shape = (n_row, columns // n_row // LANES, LANES)
    c_shape = (n_col, rows // n_col // LANES, LANES)
    zq, cq = z_shape[1], c_shape[1]
    blocks = rows // width
    any_spec = pl.BlockSpec(memory_space=pltpu.HBM)
    phases = 5 * iters + 7
    outs = pl.pallas_call(
        functools.partial(kernel, (n_row, n_col, iters, slots)),
        out_shape=(
            jax.ShapeDtypeStruct(z_shape, F32),
            jax.ShapeDtypeStruct(c_shape[1:], F32),
            jax.ShapeDtypeStruct((1, 2), F32),
        ),
        in_specs=[any_spec] * 14,
        out_specs=(any_spec,) * 3,
        scratch_shapes=[
            pltpu.VMEM((slots, width, width), BF16),
            pltpu.VMEM((slots, width, width), BF16),
            pltpu.SMEM((1, slots), jnp.int32),
            pltpu.SMEM((1, slots), jnp.int32),
            pltpu.SMEM((1,), jnp.int32),
            pltpu.SMEM((1, 2), F32),
            pltpu.VMEM((iters, columns // n_row), F32),
            pltpu.VMEM((iters, rows), F32),
            pltpu.VMEM((iters, columns), jnp.int32),
            pltpu.VMEM((iters, rows), jnp.int32),
            pltpu.VMEM(z_shape[1:], F32),
            pltpu.VMEM(c_shape[1:], F32),
            pltpu.VMEM(z_shape[1:], F32),
            pltpu.VMEM(z_shape, F32),
            pltpu.VMEM(c_shape, F32),
            pltpu.VMEM((iters, zq, LANES), F32),
            pltpu.VMEM((iters,) + z_shape, jnp.int32),
            pltpu.VMEM((iters, cq, LANES), F32),
            pltpu.VMEM((iters * blocks, slots * width), BF16),
            pltpu.VMEM((slots, width), F32),
            pltpu.VMEM((slots, width), jnp.int32),
            pltpu.VMEM(z_shape, F32),
            pltpu.VMEM(z_shape, F32),
            pltpu.VMEM((iters,) + z_shape, F32),
            pltpu.VMEM((iters, n_row - 1, zq, LANES), F32),
            pltpu.VMEM((n_row, iters, zq, LANES), F32),
            pltpu.VMEM((n_row - 1, iters, zq, LANES), F32),
            pltpu.VMEM((iters,) + z_shape, F32),
            pltpu.VMEM((iters, n_row, slots, width), BF16),
            pltpu.VMEM((iters - 1,) + z_shape, F32),
            pltpu.VMEM((n_row, iters, zq, LANES), BF16),
            pltpu.VMEM(z_shape, F32),
            pltpu.VMEM((n_row, 1, 2 * LANES), F32),
            pltpu.VMEM((rows // LANES, LANES), F32),
            pltpu.VMEM((iters,) + c_shape, F32),
            pltpu.VMEM((iters, n_col - 1, cq, LANES), F32),
            pltpu.VMEM((iters - 1,) + c_shape, F32),
            pltpu.VMEM(z_shape, F32),
            pltpu.VMEM(c_shape[1:], F32),
            pltpu.VMEM((n_row, 1, LANES), F32),
            pltpu.VMEM((n_col, 1, LANES), F32),
            pltpu.VMEM((1, 2), F32),
            pltpu.SemaphoreType.DMA((14 + slots // 8,)),
            pltpu.SemaphoreType.DMA((phases,)),
            pltpu.SemaphoreType.DMA((phases,)),
        ],
        compiler_params=pltpu.CompilerParams(
            collective_id=0, has_side_effects=True, vmem_limit_bytes=64 << 20
        ),
        name="primal_dual_adjoint",
    )(
        tile_data.reshape(slots, width, width),
        tile_row_block.reshape(1, slots),
        tile_column_block.reshape(1, slots),
        tile_count.reshape(1),
        saved_primal,
        saved_dual,
        primal_mask,
        dual_mask,
        cost_vector.reshape(z_shape),
        demand.reshape(c_shape),
        upper_bound.reshape(z_shape),
        step_sizes.reshape(1, 2),
        primal_cotangent.reshape(z_shape),
        dual_cotangent.reshape(c_shape),
    )
    padj, dadj, grad = pl.pallas_call(
        hand_over,
        out_shape=tuple(jax.ShapeDtypeStruct(out.shape, F32) for out in outs),
        in_specs=[any_spec] * 3,
        out_specs=(any_spec,) * 3,
        scratch_shapes=[pltpu.SemaphoreType.DMA((3,))],
        compiler_params=pltpu.CompilerParams(vmem_limit_bytes=64 << 20),
        name="hand_over",
    )(*outs)
    return (padj.reshape(columns), dadj.reshape(rows // n_col), grad.reshape(2))


def solution(mesh):
    placed = (
        P("row", "col", None, None, None),
        P("row", "col", None),
        P("row", "col", None),
        P("row", "col"),
        P(None, "col"),
        P(None, "row"),
        P(None, "col"),
        P(None, "row"),
        P("col"),
        P("row"),
        P("col"),
        P(),
        P("col"),
        P("row"),
    )
    return jax.shard_map(
        local,
        mesh=mesh,
        in_specs=placed,
        out_specs=(P("col"), P(("row", "col")), P()),
        check_vma=False,
    )
```

```python
import functools
import math

import jax
import jax.numpy as jnp
from jax import lax
from jax.experimental import pallas as pl
from jax.experimental.pallas import tpu as pltpu
from jax.sharding import PartitionSpec as P

F32 = jnp.float32
BF16 = jnp.bfloat16
LANES = 128
NN = (((1,), (0,)), ((), ()))
NT = (((1,), (1,)), ((), ()))


def ring_offsets(n):
    return sorted(range(1, n), key=lambda r: -min(r, n - r))


def kernel(
    dims,
    tiles_hbm,
    rb_hbm,
    cb_hbm,
    count_hbm,
    primal_hbm,
    dual_hbm,
    pmask_hbm,
    dmask_hbm,
    cost_hbm,
    demand_hbm,
    upper_hbm,
    steps_hbm,
    pcot_hbm,
    dcot_hbm,
    padj_hbm,
    dadj_hbm,
    grad_hbm,
    tiles,
    turned,
    rb_s,
    cb_s,
    count_s,
    steps_s,
    primal_in,
    dual_in,
    pmask_in,
    dmask_in,
    cost,
    demand,
    upper,
    pcot,
    dcot,
    primal,
    pmask,
    dmask,
    lhs,
    picked,
    picked_mask,
    p_rows,
    z_lin,
    z_send,
    z_recv,
    z3_send,
    z3_recv,
    hilo,
    prod_all,
    ax_all,
    x_all,
    rm_all,
    idx_all,
    c_lin,
    c_send,
    c_recv,
    d_all,
    out_all,
    dadj,
    sz_all,
    sc_all,
    grad,
    in_sem,
    send_sem,
    recv_sem,
):
    n_row, n_col, iters, slots = dims
    me_r = lax.axis_index("row")
    me_c = lax.axis_index("col")
    blocks = 64
    width = tiles.shape[-1]
    group = 8

    def fetch(i, src, dst):
        copy = pltpu.make_async_copy(src, dst, in_sem.at[i])
        copy.start()
        return copy

    z_lanes = primal_in.shape[1]
    small = [
        fetch(0, rb_hbm, rb_s),
        fetch(1, cb_hbm, cb_s),
        fetch(2, count_hbm, count_s),
        fetch(3, steps_hbm, steps_s),
        fetch(4, dmask_hbm, dmask_in),
        fetch(5, dcot_hbm, dcot),
    ]
    tile_copies = [
        fetch(14 + g, tiles_hbm.at[pl.ds(g * group, group)], tiles.at[pl.ds(g * group, group)])
        for g in range(slots // group)
    ]
    z_at = pl.ds(pl.multiple_of(me_r * z_lanes, LANES), z_lanes)
    rest = [
        fetch(6, dual_hbm, dual_in),
        fetch(7, primal_hbm.at[:, z_at], primal_in),
        fetch(8, pmask_hbm, pmask_in),
        fetch(9, cost_hbm.at[me_r], cost),
        fetch(10, upper_hbm.at[me_r], upper),
        fetch(11, pcot_hbm, pcot),
        fetch(12, demand_hbm.at[me_c], demand),
    ]

    z_peers = [(r, lax.rem(me_r + r, n_row)) for r in ring_offsets(n_row)]
    side = math.isqrt(n_col // 2)
    x, y, core = lax.div(me_c, 2 * side), lax.rem(lax.div(me_c, 2), side), lax.rem(me_c, 2)
    steps = [(dx, dy, dz) for dx in range(side) for dy in range(side) for dz in range(2)][1:]
    steps.sort(key=lambda t: -min(t[0], side - t[0]) - min(t[1], side - t[1]) - 0.5 * t[2])
    c_peers = [
        (
            i + 1,
            (lax.rem(x + dx, side) * side + lax.rem(y + dy, side)) * 2 + lax.rem(core + dz, 2),
        )
        for i, (dx, dy, dz) in enumerate(steps)
    ]
    barrier = pltpu.get_barrier_semaphore()
    for _, r in z_peers:
        pl.semaphore_signal(barrier, inc=1, device_id={"row": r})
    for _, c in c_peers:
        pl.semaphore_signal(barrier, inc=1, device_id={"col": c})

    def send(sem, src, dst, peer):
        pltpu.make_async_remote_copy(
            src_ref=src,
            dst_ref=dst,
            send_sem=send_sem.at[sem],
            recv_sem=recv_sem.at[sem],
            device_id=peer,
            device_id_type=pl.DeviceIdType.MESH,
        ).start()

    def gather_z(sem, here):
        for _, peer in z_peers:
            send(sem, here, here, {"row": peer})

    def gather_c(sem, here):
        for _, peer in c_peers:
            send(sem, here, here, {"col": peer})

    def arrive(sem, ref):
        pltpu.make_async_copy(ref, ref, recv_sem.at[sem]).wait()

    def left(sem, ref):
        pltpu.make_async_copy(ref, ref, send_sem.at[sem]).wait()

    def others(n):
        return pl.ds(0, n - 1)

    SCATTER, PROD, FOLD, DUAL, AX = range(5)

    def phase(k, which):
        return 5 * k + which

    Z3, XG, RM, OUT, SZ, SC, IDX = (5 * iters + i for i in range(7))

    for copy in small:
        copy.wait()
    tau = steps_s[0, 0]
    sigma = steps_s[0, 1]
    weights = [(k + 1.0) / (k + 2.0) for k in range(iters)]
    last = iters - 1

    iota = lax.broadcasted_iota(jnp.int32, (blocks, LANES), 0)
    iota8 = lax.broadcasted_iota(jnp.int32, (group, width), 0)

    def live_block(s, index_ref):
        return index_ref[0, s] + blocks * jnp.maximum(s + 1 - count_s[0], 0)

    def spread(s, index_ref, halves):
        keep = iota == live_block(s, index_ref)
        return [
            jnp.where(keep, jnp.broadcast_to(h, (blocks, LANES)), 0.0).astype(BF16) for h in halves
        ]

    def dot(a, b):
        return lax.dot_general(a, b, NN, preferred_element_type=F32)

    def slot_products(value, wait=None):
        hi = value.astype(BF16).astype(F32)
        lo = value - hi
        his, los = [], []
        for g in range(slots // group):
            if wait is not None:
                wait[g].wait()
            cut = slice(g * group, (g + 1) * group)
            rows = jnp.concatenate([hi[cut], lo[cut]], axis=0).astype(BF16)
            ph = jnp.zeros((group, width), F32)
            po = jnp.zeros((group, width), F32)
            for i in range(group):
                both = dot(rows, tiles[g * group + i])
                ph = jnp.where(iota8 == i, both[:group], ph)
                po = jnp.where(iota8 == i, both[group:], po)
            his.append(ph)
            los.append(po)
        return jnp.concatenate(his, axis=0), jnp.concatenate(los, axis=0)

    def scatter(hot, value):
        a = value.astype(BF16)
        r = value - a.astype(F32)
        b = r.astype(BF16)
        c = (r - b.astype(F32)).astype(BF16)
        return dot(hot, jnp.concatenate([a, b, c, jnp.zeros_like(a)], axis=0))

    def apply_duals():
        for s in range(slots):
            r = rb_s[0, s]
            for v in range(iters):
                halves = [dual_in[pl.ds(v, 1), pl.ds((2 * r + h) * LANES, LANES)] for h in range(2)]
                for h, value in enumerate(spread(s, cb_s, halves)):
                    lhs[
                        v * blocks : (v + 1) * blocks,
                        s * width + h * LANES : s * width + (h + 1) * LANES,
                    ] = value
        return dot(lhs[...], tiles[...].reshape(slots * width, width))

    def apply_forward():
        acc = jnp.zeros((blocks, width), F32)
        for s in range(slots):
            c = cb_s[0, s]
            b = lax.div(c, 8)
            i = 2 * lax.rem(c, 8)
            halves = [p_rows[b, pl.ds(i, 1), :], p_rows[b, pl.ds(i + 1, 1), :]]
            row = jnp.concatenate(spread(s, rb_s, halves), axis=1)
            acc = acc + dot(row, turned[s])
        return acc

    def store_z(dst, value):
        for j in range(n_row):
            for h in range(2):
                dst[j, pl.ds(h, 8, stride=2), :] = value[
                    8 * j : 8 * j + 8, h * LANES : (h + 1) * LANES
                ]

    def send_exact(k):
        for r, peer in z_peers:
            send(phase(k, SCATTER), z_send.at[k, peer], z_recv.at[k, r - 1], {"row": peer})

    for s in range(slots):
        r = rb_s[0, s]
        a = lax.div(r, 2)
        b = 2 * lax.rem(r, 2)
        for h in range(2):
            cut = slice(h * LANES, (h + 1) * LANES)
            picked[s : s + 1, cut] = dcot[a, pl.ds(b + h, 1), :]
            picked_mask[s : s + 1, cut] = dmask_in[pl.ds(last, 1), pl.ds((2 * r + h) * LANES, LANES)]
    start = picked_mask[...].astype(F32) * weights[last] * picked[...]

    tau_local = jnp.zeros((), F32)
    sigma_local = jnp.zeros((), F32)
    anchor_x = anchor_y = None
    ax = ay = d = None
    hot = hot_all = None

    for k in reversed(range(iters)):
        weight = weights[k]
        if k == last:
            ph, po = slot_products(start, tile_copies)
        else:
            for s in range(slots):
                r = rb_s[0, s]
                a = lax.div(r, 2)
                b = 2 * lax.rem(r, 2)
                for h in range(2):
                    cut = slice(h * LANES, (h + 1) * LANES)
                    picked[s : s + 1, cut] = d_all[k, a, pl.ds(b + h, 1), :]
            ph, po = slot_products(picked[...])
        prod_all[k, me_r] = ph.astype(BF16)
        if k == last:
            lane2 = lax.broadcasted_iota(jnp.int32, (1, 2 * LANES), 1)
            lane = lax.broadcasted_iota(jnp.int32, (1, LANES), 1)
            mine = jnp.full((1, 2 * LANES), -1, jnp.int32)
            own = jnp.full((1, LANES), -1, jnp.int32)
            for s in range(slots):
                block = live_block(s, cb_s)
                mine = jnp.where(lane2 == me_r * slots + s, block, mine)
                own = jnp.where(lax.rem(lane, slots) == s, block, own)
            idx_all[me_r] = mine.astype(F32)
            hot = jnp.where(iota == own, 1.0, 0.0).astype(BF16)
            pl.semaphore_wait(barrier, len(z_peers) + len(c_peers))
        gather_z(phase(k, PROD), prod_all.at[k, me_r])
        if k == last:
            gather_z(IDX, idx_all.at[me_r])
        store_z(z_send.at[k], scatter(hot, ph))
        if k == 0:
            send_exact(k)
        store_z(hilo.at[k], scatter(hot, ph + po))
        if k == last:
            for copy in rest:
                copy.wait()
            duals = apply_duals()
            for i in range(iters):
                for j in range(n_row):
                    for h in range(2):
                        z3_send[j, i, pl.ds(h, 8, stride=2), :] = duals[
                            i * blocks + 8 * j : i * blocks + 8 * j + 8,
                            h * LANES : (h + 1) * LANES,
                        ]
            for i in range(iters):
                for j in range(n_row):
                    for q in range(16):
                        at = (16 * j + q) * LANES
                        pmask[i, j, q : q + 1, :] = pmask_in[i : i + 1, at : at + LANES]
                for q in range(16):
                    primal[i, q : q + 1, :] = primal_in[i : i + 1, q * LANES : (q + 1) * LANES]
                for q in range(4):
                    at = pl.multiple_of(me_c * (4 * LANES) + q * LANES, LANES)
                    dmask[i, q : q + 1, :] = dmask_in[i : i + 1, pl.ds(at, LANES)].astype(F32)
            for s in range(slots):
                turned[s] = tiles[s].T
            ax = pcot[me_r]
            ay = dcot[me_c]
            anchor_x = (1.0 - weight) * ax
            anchor_y = (1.0 - weight) * ay
            d = dmask[k] * weight * ay
        else:
            if k == last - 1:
                arrive(XG, x_all.at[others(n_row)])
                arrive(RM, rm_all.at[others(n_row)])
                sigma_local = sigma_local - jnp.sum(hilo[last] * x_all[:, last].astype(F32))
            sigma_local = sigma_local - jnp.sum(hilo[k] * x_all[:, k].astype(F32))
        sigma_local = sigma_local + jnp.sum(d * demand[...])
        if k == 0:
            held = pmask[0, me_r].astype(F32) * weight * ax * primal[0]
            tau_local = tau_local - jnp.sum(held) + (2.0 * sigma) * jnp.sum(z_send[0] * rm_all[...])
            lane = lax.broadcasted_iota(jnp.int32, (1, LANES), 1)
            sz_all[me_r] = jnp.where(lane == 0, tau_local, jnp.where(lane == 1, sigma_local, 0.0))
            gather_z(SZ, sz_all.at[me_r])
        if k == last:
            arrive(IDX, idx_all.at[others(n_row)])
            index = idx_all[0]
            for r in range(1, n_row):
                index = jnp.maximum(index, idx_all[r])
            rows = lax.broadcasted_iota(jnp.int32, (blocks, 2 * LANES), 0).astype(F32)
            hot_all = jnp.where(rows == index, 1.0, 0.0).astype(BF16)
            ax_full = pcot[...]
        else:
            arrive(phase(k + 1, AX), ax_all.at[k, others(n_row)])
            ax_full = ax_all[k]
        arrive(phase(k, PROD), prod_all.at[k, others(n_row)])
        if k > 0:
            send_exact(k)
        store_z(z_lin, dot(hot_all, prod_all[k].reshape(n_row * slots, width)))
        p_full = pmask[k].astype(F32) * (weight * ax_full - (2.0 * sigma) * z_lin[...])
        p_rows[...] = p_full.astype(BF16).astype(F32)
        if k == last:
            for r, peer in z_peers:
                send(Z3, z3_send.at[peer], z3_recv.at[r - 1], {"row": peer})
        image = apply_forward()
        c_lin[pl.ds(0, blocks, stride=2), :] = image[:, :LANES]
        c_lin[pl.ds(1, blocks, stride=2), :] = image[:, LANES:]
        c_send[k] = c_lin[...].reshape(n_col, 4, LANES)
        for r, peer in c_peers:
            send(phase(k, FOLD), c_send.at[k, peer], c_recv.at[k, r - 1], {"col": peer})
        if k == 0:
            arrive(SZ, sz_all.at[others(n_row)])
            total = sz_all[0]
            for r in range(1, n_row):
                total = total + sz_all[r]
            sc_all[me_c] = total
            gather_c(SC, sc_all.at[me_c])
        arrive(phase(k, SCATTER), z_recv.at[k])
        back = z_send[k, me_r]
        for r in range(n_row - 1):
            back = back + z_recv[k, r]
        if k != last:
            anchor_x = anchor_x + (1.0 - weight) * ax
        p = pmask[k, me_r].astype(F32) * (weight * ax - (2.0 * sigma) * back)
        ax = p + sigma * back
        if k > 0:
            ax_all[k - 1, me_r] = ax
            gather_z(phase(k, AX), ax_all.at[k - 1, me_r])
        else:
            out_all[me_r] = ax + anchor_x
            gather_z(OUT, out_all.at[me_r])
        if k == last:
            p_last = p
        elif k > 0:
            tau_local = tau_local - jnp.sum(p * primal[k])
        arrive(phase(k, FOLD), c_recv.at[k])
        rows = c_send[k, me_c]
        for r in range(n_col - 1):
            rows = rows + c_recv[k, r]
        ay = d + tau * rows
        if k > 0:
            weight = weights[k - 1]
            anchor_y = anchor_y + (1.0 - weight) * ay
            d = dmask[k - 1] * weight * ay
            d_all[k - 1, me_c] = d
            gather_c(phase(k - 1, DUAL), d_all.at[k - 1, me_c])
            if k == last:
                arrive(Z3, z3_recv)
                for i in range(iters):
                    column = z3_send[me_r, i]
                    for r in range(n_row - 1):
                        column = column + z3_recv[r, i]
                    reduced = cost[...] - column
                    saved = primal[i]
                    half = jnp.minimum(jnp.maximum(saved - tau * reduced, 0.0), upper[...])
                    x_all[me_r, i] = (2.0 * half - saved).astype(BF16)
                    primal[i] = reduced
                rm_all[me_r] = pmask[0, me_r].astype(F32) * primal[0]
                gather_z(XG, x_all.at[me_r])
                gather_z(RM, rm_all.at[me_r])
                tau_local = tau_local - jnp.sum(p_last * primal[last])
            arrive(phase(k - 1, DUAL), d_all.at[k - 1, others(n_col)])

    dadj[...] = ay + anchor_y
    dadj_copy = pltpu.make_async_copy(dadj, dadj_hbm, in_sem.at[1])
    dadj_copy.start()
    arrive(OUT, out_all.at[others(n_row)])
    padj_copy = pltpu.make_async_copy(out_all, padj_hbm, in_sem.at[0])
    padj_copy.start()
    arrive(SC, sc_all.at[others(n_col)])
    total = sc_all[0]
    for c in range(1, n_col):
        total = total + sc_all[c]
    lane = lax.broadcasted_iota(jnp.int32, (1, LANES), 1)
    columns = float(n_col * blocks * width)
    lines = float(n_row * blocks * width)
    scaled = total * jnp.where(lane == 0, 1.0 / math.sqrt(columns), 1.0 / math.sqrt(lines))
    grad[...] = scaled[:, :2]
    grad_copy = pltpu.make_async_copy(grad, grad_hbm, in_sem.at[2])
    grad_copy.start()

    for k in range(iters):
        left(phase(k, SCATTER), z_recv.at[k])
        left(phase(k, PROD), prod_all.at[k, others(n_row)])
        left(phase(k, FOLD), c_recv.at[k])
        if k < last:
            left(phase(k, DUAL), d_all.at[k, others(n_col)])
        if k > 0:
            left(phase(k, AX), ax_all.at[k - 1, others(n_row)])
    left(Z3, z3_recv)
    left(XG, x_all.at[others(n_row)])
    left(RM, rm_all.at[others(n_row)])
    left(IDX, idx_all.at[others(n_row)])
    left(OUT, out_all.at[others(n_row)])
    left(SZ, sz_all.at[others(n_row)])
    left(SC, sc_all.at[others(n_col)])
    padj_copy.wait()
    dadj_copy.wait()
    grad_copy.wait()


def hand_over(padj_in, dadj_in, grad_in, padj, dadj, grad, padj_v, dadj_v, grad_v, sem):
    copies = [
        pltpu.make_async_copy(src, dst, sem.at[i])
        for i, (src, dst) in enumerate(((padj_in, padj_v), (dadj_in, dadj_v), (grad_in, grad_v)))
    ]
    for copy in copies:
        copy.start()
    outs = [
        pltpu.make_async_copy(src, dst, sem.at[3 + i])
        for i, (src, dst) in enumerate(((padj_v, padj), (dadj_v, dadj), (grad_v, grad)))
    ]
    for copy, out in zip(copies, outs):
        copy.wait()
        out.start()
    for out in outs:
        out.wait()


def local(
    tile_data,
    tile_row_block,
    tile_column_block,
    tile_count,
    saved_primal,
    saved_dual,
    primal_mask,
    dual_mask,
    cost_vector,
    demand,
    upper_bound,
    step_sizes,
    primal_cotangent,
    dual_cotangent,
):
    n_row = lax.axis_size("row")
    n_col = lax.axis_size("col")
    slots, width = tile_data.shape[2], tile_data.shape[-1]
    iters = saved_primal.shape[0]
    rows = saved_dual.shape[1]
    columns = saved_primal.shape[1]
    z_shape = (n_row, columns // n_row // LANES, LANES)
    c_shape = (n_col, rows // n_col // LANES, LANES)
    zq, cq = z_shape[1], c_shape[1]
    blocks = rows // width
    any_spec = pl.BlockSpec(memory_space=pltpu.HBM)
    phases = 5 * iters + 7
    outs = pl.pallas_call(
        functools.partial(kernel, (n_row, n_col, iters, slots)),
        out_shape=(
            jax.ShapeDtypeStruct(z_shape, F32),
            jax.ShapeDtypeStruct(c_shape[1:], F32),
            jax.ShapeDtypeStruct((1, 2), F32),
        ),
        in_specs=[any_spec] * 14,
        out_specs=(any_spec,) * 3,
        scratch_shapes=[
            pltpu.VMEM((slots, width, width), BF16),
            pltpu.VMEM((slots, width, width), BF16),
            pltpu.SMEM((1, slots), jnp.int32),
            pltpu.SMEM((1, slots), jnp.int32),
            pltpu.SMEM((1,), jnp.int32),
            pltpu.SMEM((1, 2), F32),
            pltpu.VMEM((iters, columns // n_row), F32),
            pltpu.VMEM((iters, rows), F32),
            pltpu.VMEM((iters, columns), jnp.int32),
            pltpu.VMEM((iters, rows), jnp.int32),
            pltpu.VMEM(z_shape[1:], F32),
            pltpu.VMEM(c_shape[1:], F32),
            pltpu.VMEM(z_shape[1:], F32),
            pltpu.VMEM(z_shape, F32),
            pltpu.VMEM(c_shape, F32),
            pltpu.VMEM((iters, zq, LANES), F32),
            pltpu.VMEM((iters,) + z_shape, jnp.int32),
            pltpu.VMEM((iters, cq, LANES), F32),
            pltpu.VMEM((iters * blocks, slots * width), BF16),
            pltpu.VMEM((slots, width), F32),
            pltpu.VMEM((slots, width), jnp.int32),
            pltpu.VMEM(z_shape, F32),
            pltpu.VMEM(z_shape, F32),
            pltpu.VMEM((iters,) + z_shape, F32),
            pltpu.VMEM((iters, n_row - 1, zq, LANES), F32),
            pltpu.VMEM((n_row, iters, zq, LANES), F32),
            pltpu.VMEM((n_row - 1, iters, zq, LANES), F32),
            pltpu.VMEM((iters,) + z_shape, F32),
            pltpu.VMEM((iters, n_row, slots, width), BF16),
            pltpu.VMEM((iters - 1,) + z_shape, F32),
            pltpu.VMEM((n_row, iters, zq, LANES), BF16),
            pltpu.VMEM(z_shape, F32),
            pltpu.VMEM((n_row, 1, 2 * LANES), F32),
            pltpu.VMEM((rows // LANES, LANES), F32),
            pltpu.VMEM((iters,) + c_shape, F32),
            pltpu.VMEM((iters, n_col - 1, cq, LANES), F32),
            pltpu.VMEM((iters - 1,) + c_shape, F32),
            pltpu.VMEM(z_shape, F32),
            pltpu.VMEM(c_shape[1:], F32),
            pltpu.VMEM((n_row, 1, LANES), F32),
            pltpu.VMEM((n_col, 1, LANES), F32),
            pltpu.VMEM((1, 2), F32),
            pltpu.SemaphoreType.DMA((14 + slots // 8,)),
            pltpu.SemaphoreType.DMA((phases,)),
            pltpu.SemaphoreType.DMA((phases,)),
        ],
        compiler_params=pltpu.CompilerParams(
            collective_id=0, has_side_effects=True, vmem_limit_bytes=64 << 20
        ),
        name="primal_dual_adjoint",
    )(
        tile_data.reshape(slots, width, width),
        tile_row_block.reshape(1, slots),
        tile_column_block.reshape(1, slots),
        tile_count.reshape(1),
        saved_primal,
        saved_dual,
        primal_mask,
        dual_mask,
        cost_vector.reshape(z_shape),
        demand.reshape(c_shape),
        upper_bound.reshape(z_shape),
        step_sizes.reshape(1, 2),
        primal_cotangent.reshape(z_shape),
        dual_cotangent.reshape(c_shape),
    )
    padj, dadj, grad = pl.pallas_call(
        hand_over,
        out_shape=tuple(jax.ShapeDtypeStruct(out.shape, F32) for out in outs),
        in_specs=[any_spec] * 3,
        out_specs=(any_spec,) * 3,
        scratch_shapes=[pltpu.VMEM(out.shape, F32) for out in outs] + [pltpu.SemaphoreType.DMA((6,))],
        compiler_params=pltpu.CompilerParams(vmem_limit_bytes=64 << 20),
        name="hand_over",
    )(*outs)
    return (padj.reshape(columns), dadj.reshape(rows // n_col), grad.reshape(2))


def solution(mesh):
    placed = (
        P("row", "col", None, None, None),
        P("row", "col", None),
        P("row", "col", None),
        P("row", "col"),
        P(None, "col"),
        P(None, "row"),
        P(None, "col"),
        P(None, "row"),
        P("col"),
        P("row"),
        P("col"),
        P(),
        P("col"),
        P("row"),
    )
    return jax.shard_map(
        local,
        mesh=mesh,
        in_specs=placed,
        out_specs=(P("col"), P(("row", "col")), P()),
        check_vma=False,
    )
```

```python
import functools
import math

import jax
import jax.numpy as jnp
from jax import lax
from jax.experimental import pallas as pl
from jax.experimental.pallas import tpu as pltpu
from jax.sharding import PartitionSpec as P

F32 = jnp.float32
BF16 = jnp.bfloat16
LANES = 128
NN = (((1,), (0,)), ((), ()))
NT = (((1,), (1,)), ((), ()))


def ring_offsets(n):
    return sorted(range(1, n), key=lambda r: -min(r, n - r))


def kernel(
    dims,
    tiles_hbm,
    rb_hbm,
    cb_hbm,
    count_hbm,
    primal_hbm,
    dual_hbm,
    pmask_hbm,
    dmask_hbm,
    cost_hbm,
    demand_hbm,
    upper_hbm,
    steps_hbm,
    pcot_hbm,
    dcot_hbm,
    padj_hbm,
    dadj_hbm,
    grad_hbm,
    tiles,
    turned,
    rb_s,
    cb_s,
    count_s,
    steps_s,
    primal_in,
    dual_in,
    pmask_in,
    dmask_in,
    cost,
    demand,
    upper,
    pcot,
    dcot,
    primal,
    pmask,
    dmask,
    lhs,
    picked,
    picked_mask,
    p_rows,
    z_lin,
    z_send,
    z_recv,
    z3_send,
    z3_recv,
    hilo,
    prod_all,
    ax_all,
    x_all,
    rm_all,
    idx_all,
    c_lin,
    c_send,
    c_recv,
    d_all,
    out_all,
    dadj,
    sz_all,
    sc_all,
    grad,
    in_sem,
    send_sem,
    recv_sem,
):
    n_row, n_col, iters, slots = dims
    me_r = lax.axis_index("row")
    me_c = lax.axis_index("col")
    blocks = 64
    width = tiles.shape[-1]
    group = 8

    def fetch(i, src, dst):
        copy = pltpu.make_async_copy(src, dst, in_sem.at[i])
        copy.start()
        return copy

    z_lanes = primal_in.shape[1]
    small = [
        fetch(0, rb_hbm, rb_s),
        fetch(1, cb_hbm, cb_s),
        fetch(2, count_hbm, count_s),
        fetch(3, steps_hbm, steps_s),
        fetch(4, dmask_hbm, dmask_in),
        fetch(5, dcot_hbm, dcot),
    ]
    tile_copies = [
        fetch(14 + g, tiles_hbm.at[pl.ds(g * group, group)], tiles.at[pl.ds(g * group, group)])
        for g in range(slots // group)
    ]
    z_at = pl.ds(pl.multiple_of(me_r * z_lanes, LANES), z_lanes)
    rest = [
        fetch(6, dual_hbm, dual_in),
        fetch(7, primal_hbm.at[:, z_at], primal_in),
        fetch(8, pmask_hbm, pmask_in),
        fetch(9, cost_hbm.at[me_r], cost),
        fetch(10, upper_hbm.at[me_r], upper),
        fetch(11, pcot_hbm, pcot),
        fetch(12, demand_hbm.at[me_c], demand),
    ]

    z_peers = [(r, lax.rem(me_r + r, n_row)) for r in ring_offsets(n_row)]
    side = math.isqrt(n_col // 2)
    x, y, core = lax.div(me_c, 2 * side), lax.rem(lax.div(me_c, 2), side), lax.rem(me_c, 2)
    steps = [(dx, dy, dz) for dx in range(side) for dy in range(side) for dz in range(2)][1:]
    steps.sort(key=lambda t: -min(t[0], side - t[0]) - min(t[1], side - t[1]) - 0.5 * t[2])
    c_peers = [
        (
            i + 1,
            (lax.rem(x + dx, side) * side + lax.rem(y + dy, side)) * 2 + lax.rem(core + dz, 2),
        )
        for i, (dx, dy, dz) in enumerate(steps)
    ]
    barrier = pltpu.get_barrier_semaphore()
    for _, r in z_peers:
        pl.semaphore_signal(barrier, inc=1, device_id={"row": r})
    for _, c in c_peers:
        pl.semaphore_signal(barrier, inc=1, device_id={"col": c})

    def send(sem, src, dst, peer):
        pltpu.make_async_remote_copy(
            src_ref=src,
            dst_ref=dst,
            send_sem=send_sem.at[sem],
            recv_sem=recv_sem.at[sem],
            device_id=peer,
            device_id_type=pl.DeviceIdType.MESH,
        ).start()

    def gather_z(sem, here):
        for _, peer in z_peers:
            send(sem, here, here, {"row": peer})

    def gather_c(sem, here):
        for _, peer in c_peers:
            send(sem, here, here, {"col": peer})

    def arrive(sem, ref):
        pltpu.make_async_copy(ref, ref, recv_sem.at[sem]).wait()

    def left(sem, ref):
        pltpu.make_async_copy(ref, ref, send_sem.at[sem]).wait()

    def others(n):
        return pl.ds(0, n - 1)

    SCATTER, PROD, FOLD, DUAL, AX = range(5)

    def phase(k, which):
        return 5 * k + which

    Z3, XG, RM, OUT, SZ, SC, IDX = (5 * iters + i for i in range(7))

    for copy in small:
        copy.wait()
    tau = steps_s[0, 0]
    sigma = steps_s[0, 1]
    weights = [(k + 1.0) / (k + 2.0) for k in range(iters)]
    last = iters - 1

    iota = lax.broadcasted_iota(jnp.int32, (blocks, LANES), 0)
    iota8 = lax.broadcasted_iota(jnp.int32, (group, width), 0)

    def live_block(s, index_ref):
        return index_ref[0, s] + blocks * jnp.maximum(s + 1 - count_s[0], 0)

    def spread(s, index_ref, halves):
        keep = iota == live_block(s, index_ref)
        return [
            jnp.where(keep, jnp.broadcast_to(h, (blocks, LANES)), 0.0).astype(BF16) for h in halves
        ]

    def dot(a, b):
        return lax.dot_general(a, b, NN, preferred_element_type=F32)

    def slot_products(value, wait=None):
        hi = value.astype(BF16).astype(F32)
        lo = value - hi
        his, los = [], []
        for g in range(slots // group):
            if wait is not None:
                wait[g].wait()
            cut = slice(g * group, (g + 1) * group)
            rows = jnp.concatenate([hi[cut], lo[cut]], axis=0).astype(BF16)
            ph = jnp.zeros((group, width), F32)
            po = jnp.zeros((group, width), F32)
            for i in range(group):
                both = dot(rows, tiles[g * group + i])
                ph = jnp.where(iota8 == i, both[:group], ph)
                po = jnp.where(iota8 == i, both[group:], po)
            his.append(ph)
            los.append(po)
        return jnp.concatenate(his, axis=0), jnp.concatenate(los, axis=0)

    def scatter(hot, value):
        a = value.astype(BF16)
        r = value - a.astype(F32)
        b = r.astype(BF16)
        c = (r - b.astype(F32)).astype(BF16)
        return dot(hot, jnp.concatenate([a, b, c, jnp.zeros_like(a)], axis=0))

    def apply_duals():
        for s in range(slots):
            r = rb_s[0, s]
            for v in range(iters):
                halves = [dual_in[pl.ds(v, 1), pl.ds((2 * r + h) * LANES, LANES)] for h in range(2)]
                for h, value in enumerate(spread(s, cb_s, halves)):
                    lhs[
                        v * blocks : (v + 1) * blocks,
                        s * width + h * LANES : s * width + (h + 1) * LANES,
                    ] = value
        return dot(lhs[...], tiles[...].reshape(slots * width, width))

    def apply_forward():
        acc = jnp.zeros((blocks, width), F32)
        for s in range(slots):
            c = cb_s[0, s]
            b = lax.div(c, 8)
            i = 2 * lax.rem(c, 8)
            halves = [p_rows[b, pl.ds(i, 1), :], p_rows[b, pl.ds(i + 1, 1), :]]
            row = jnp.concatenate(spread(s, rb_s, halves), axis=1)
            acc = acc + dot(row, turned[s])
        return acc

    def store_z(dst, value):
        for j in range(n_row):
            for h in range(2):
                dst[j, pl.ds(h, 8, stride=2), :] = value[
                    8 * j : 8 * j + 8, h * LANES : (h + 1) * LANES
                ]

    def send_exact(k):
        for r, peer in z_peers:
            send(phase(k, SCATTER), z_send.at[k, peer], z_recv.at[k, r - 1], {"row": peer})

    for s in range(slots):
        r = rb_s[0, s]
        a = lax.div(r, 2)
        b = 2 * lax.rem(r, 2)
        for h in range(2):
            cut = slice(h * LANES, (h + 1) * LANES)
            picked[s : s + 1, cut] = dcot[a, pl.ds(b + h, 1), :]
            picked_mask[s : s + 1, cut] = dmask_in[pl.ds(last, 1), pl.ds((2 * r + h) * LANES, LANES)]
    start = picked_mask[...].astype(F32) * weights[last] * picked[...]

    lane2 = lax.broadcasted_iota(jnp.int32, (1, 2 * LANES), 1)
    lane = lax.broadcasted_iota(jnp.int32, (1, LANES), 1)
    mine = jnp.full((1, 2 * LANES), -1, jnp.int32)
    own = jnp.full((1, LANES), -1, jnp.int32)
    for s in range(slots):
        block = live_block(s, cb_s)
        mine = jnp.where(lane2 == me_r * slots + s, block, mine)
        own = jnp.where(lax.rem(lane, slots) == s, block, own)
    idx_all[me_r] = mine.astype(F32)
    hot = jnp.where(iota == own, 1.0, 0.0).astype(BF16)

    tau_local = jnp.zeros((), F32)
    sigma_local = jnp.zeros((), F32)
    anchor_x = anchor_y = None
    ax = ay = d = None
    hot_all = None

    for k in reversed(range(iters)):
        weight = weights[k]
        if k == last:
            ph, po = slot_products(start, tile_copies)
        else:
            for s in range(slots):
                r = rb_s[0, s]
                a = lax.div(r, 2)
                b = 2 * lax.rem(r, 2)
                for h in range(2):
                    cut = slice(h * LANES, (h + 1) * LANES)
                    picked[s : s + 1, cut] = d_all[k, a, pl.ds(b + h, 1), :]
            ph, po = slot_products(picked[...])
        prod_all[k, me_r] = ph.astype(BF16)
        if k == last:
            pl.semaphore_wait(barrier, len(z_peers) + len(c_peers))
            gather_z(IDX, idx_all.at[me_r])
        gather_z(phase(k, PROD), prod_all.at[k, me_r])
        store_z(z_send.at[k], scatter(hot, ph))
        store_z(hilo.at[k], scatter(hot, ph + po))
        if k == last:
            for copy in rest:
                copy.wait()
            duals = apply_duals()
            for i in range(iters):
                for j in range(n_row):
                    for h in range(2):
                        z3_send[j, i, pl.ds(h, 8, stride=2), :] = duals[
                            i * blocks + 8 * j : i * blocks + 8 * j + 8,
                            h * LANES : (h + 1) * LANES,
                        ]
            for i in range(iters):
                for j in range(n_row):
                    for q in range(16):
                        at = (16 * j + q) * LANES
                        pmask[i, j, q : q + 1, :] = pmask_in[i : i + 1, at : at + LANES]
                for q in range(16):
                    primal[i, q : q + 1, :] = primal_in[i : i + 1, q * LANES : (q + 1) * LANES]
                for q in range(4):
                    at = pl.multiple_of(me_c * (4 * LANES) + q * LANES, LANES)
                    dmask[i, q : q + 1, :] = dmask_in[i : i + 1, pl.ds(at, LANES)].astype(F32)
            for s in range(slots):
                turned[s] = tiles[s].T
            ax = pcot[me_r]
            ay = dcot[me_c]
            anchor_x = (1.0 - weight) * ax
            anchor_y = (1.0 - weight) * ay
            d = dmask[k] * weight * ay
        else:
            if k == last - 1:
                arrive(XG, x_all.at[others(n_row)])
                arrive(RM, rm_all.at[others(n_row)])
                sigma_local = sigma_local - jnp.sum(hilo[last] * x_all[:, last].astype(F32))
            sigma_local = sigma_local - jnp.sum(hilo[k] * x_all[:, k].astype(F32))
        sigma_local = sigma_local + jnp.sum(d * demand[...])
        if k == 0:
            held = pmask[0, me_r].astype(F32) * weight * ax * primal[0]
            tau_local = tau_local - jnp.sum(held) + (2.0 * sigma) * jnp.sum(z_send[0] * rm_all[...])
            lane = lax.broadcasted_iota(jnp.int32, (1, LANES), 1)
            sz_all[me_r] = jnp.where(lane == 0, tau_local, jnp.where(lane == 1, sigma_local, 0.0))
            gather_z(SZ, sz_all.at[me_r])
            send_exact(k)
        if k == last:
            arrive(IDX, idx_all.at[others(n_row)])
            index = idx_all[0]
            for r in range(1, n_row):
                index = jnp.maximum(index, idx_all[r])
            rows = lax.broadcasted_iota(jnp.int32, (blocks, 2 * LANES), 0).astype(F32)
            hot_all = jnp.where(rows == index, 1.0, 0.0).astype(BF16)
            ax_full = pcot[...]
        else:
            arrive(phase(k + 1, AX), ax_all.at[k, others(n_row)])
            ax_full = ax_all[k]
        arrive(phase(k, PROD), prod_all.at[k, others(n_row)])
        if k > 0:
            send_exact(k)
        store_z(z_lin, dot(hot_all, prod_all[k].reshape(n_row * slots, width)))
        p_full = pmask[k].astype(F32) * (weight * ax_full - (2.0 * sigma) * z_lin[...])
        p_rows[...] = p_full.astype(BF16).astype(F32)
        if k == last:
            for r, peer in z_peers:
                send(Z3, z3_send.at[peer], z3_recv.at[r - 1], {"row": peer})
        image = apply_forward()
        c_lin[pl.ds(0, blocks, stride=2), :] = image[:, :LANES]
        c_lin[pl.ds(1, blocks, stride=2), :] = image[:, LANES:]
        c_send[k] = c_lin[...].reshape(n_col, 4, LANES)
        for r, peer in c_peers:
            send(phase(k, FOLD), c_send.at[k, peer], c_recv.at[k, r - 1], {"col": peer})
        if k == 0:
            arrive(SZ, sz_all.at[others(n_row)])
            total = sz_all[0]
            for r in range(1, n_row):
                total = total + sz_all[r]
            sc_all[me_c] = total
            gather_c(SC, sc_all.at[me_c])
        arrive(phase(k, SCATTER), z_recv.at[k])
        back = z_send[k, me_r]
        for r in range(n_row - 1):
            back = back + z_recv[k, r]
        if k != last:
            anchor_x = anchor_x + (1.0 - weight) * ax
        p = pmask[k, me_r].astype(F32) * (weight * ax - (2.0 * sigma) * back)
        ax = p + sigma * back
        if k > 0:
            ax_all[k - 1, me_r] = ax
            gather_z(phase(k, AX), ax_all.at[k - 1, me_r])
        else:
            out_all[me_r] = ax + anchor_x
            gather_z(OUT, out_all.at[me_r])
        if k == last:
            p_last = p
        elif k > 0:
            tau_local = tau_local - jnp.sum(p * primal[k])
        arrive(phase(k, FOLD), c_recv.at[k])
        rows = c_send[k, me_c]
        for r in range(n_col - 1):
            rows = rows + c_recv[k, r]
        ay = d + tau * rows
        if k > 0:
            weight = weights[k - 1]
            anchor_y = anchor_y + (1.0 - weight) * ay
            d = dmask[k - 1] * weight * ay
            d_all[k - 1, me_c] = d
            gather_c(phase(k - 1, DUAL), d_all.at[k - 1, me_c])
            if k == last:
                arrive(Z3, z3_recv)
                for i in range(iters):
                    column = z3_send[me_r, i]
                    for r in range(n_row - 1):
                        column = column + z3_recv[r, i]
                    reduced = cost[...] - column
                    saved = primal[i]
                    half = jnp.minimum(jnp.maximum(saved - tau * reduced, 0.0), upper[...])
                    x_all[me_r, i] = (2.0 * half - saved).astype(BF16)
                    primal[i] = reduced
                rm_all[me_r] = pmask[0, me_r].astype(F32) * primal[0]
                gather_z(XG, x_all.at[me_r])
                gather_z(RM, rm_all.at[me_r])
                tau_local = tau_local - jnp.sum(p_last * primal[last])
            arrive(phase(k - 1, DUAL), d_all.at[k - 1, others(n_col)])

    dadj[...] = ay + anchor_y
    dadj_copy = pltpu.make_async_copy(dadj, dadj_hbm, in_sem.at[1])
    dadj_copy.start()
    arrive(OUT, out_all.at[others(n_row)])
    padj_copy = pltpu.make_async_copy(out_all, padj_hbm, in_sem.at[0])
    padj_copy.start()
    arrive(SC, sc_all.at[others(n_col)])
    total = sc_all[0]
    for c in range(1, n_col):
        total = total + sc_all[c]
    lane = lax.broadcasted_iota(jnp.int32, (1, LANES), 1)
    columns = float(n_col * blocks * width)
    lines = float(n_row * blocks * width)
    scaled = total * jnp.where(lane == 0, 1.0 / math.sqrt(columns), 1.0 / math.sqrt(lines))
    grad[...] = scaled[:, :2]
    grad_copy = pltpu.make_async_copy(grad, grad_hbm, in_sem.at[2])
    grad_copy.start()

    for k in range(iters):
        left(phase(k, SCATTER), z_recv.at[k])
        left(phase(k, PROD), prod_all.at[k, others(n_row)])
        left(phase(k, FOLD), c_recv.at[k])
        if k < last:
            left(phase(k, DUAL), d_all.at[k, others(n_col)])
        if k > 0:
            left(phase(k, AX), ax_all.at[k - 1, others(n_row)])
    left(Z3, z3_recv)
    left(XG, x_all.at[others(n_row)])
    left(RM, rm_all.at[others(n_row)])
    left(IDX, idx_all.at[others(n_row)])
    left(OUT, out_all.at[others(n_row)])
    left(SZ, sz_all.at[others(n_row)])
    left(SC, sc_all.at[others(n_col)])
    padj_copy.wait()
    dadj_copy.wait()
    grad_copy.wait()


def hand_over(padj_in, dadj_in, grad_in, padj, dadj, grad, padj_v, dadj_v, grad_v, sem):
    copies = [
        pltpu.make_async_copy(src, dst, sem.at[i])
        for i, (src, dst) in enumerate(((padj_in, padj_v), (dadj_in, dadj_v), (grad_in, grad_v)))
    ]
    for copy in copies:
        copy.start()
    outs = [
        pltpu.make_async_copy(src, dst, sem.at[3 + i])
        for i, (src, dst) in enumerate(((padj_v, padj), (dadj_v, dadj), (grad_v, grad)))
    ]
    for copy, out in zip(copies, outs):
        copy.wait()
        out.start()
    for out in outs:
        out.wait()


def local(
    tile_data,
    tile_row_block,
    tile_column_block,
    tile_count,
    saved_primal,
    saved_dual,
    primal_mask,
    dual_mask,
    cost_vector,
    demand,
    upper_bound,
    step_sizes,
    primal_cotangent,
    dual_cotangent,
):
    n_row = lax.axis_size("row")
    n_col = lax.axis_size("col")
    slots, width = tile_data.shape[2], tile_data.shape[-1]
    iters = saved_primal.shape[0]
    rows = saved_dual.shape[1]
    columns = saved_primal.shape[1]
    z_shape = (n_row, columns // n_row // LANES, LANES)
    c_shape = (n_col, rows // n_col // LANES, LANES)
    zq, cq = z_shape[1], c_shape[1]
    blocks = rows // width
    any_spec = pl.BlockSpec(memory_space=pltpu.HBM)
    phases = 5 * iters + 7
    outs = pl.pallas_call(
        functools.partial(kernel, (n_row, n_col, iters, slots)),
        out_shape=(
            jax.ShapeDtypeStruct(z_shape, F32),
            jax.ShapeDtypeStruct(c_shape[1:], F32),
            jax.ShapeDtypeStruct((1, 2), F32),
        ),
        in_specs=[any_spec] * 14,
        out_specs=(any_spec,) * 3,
        scratch_shapes=[
            pltpu.VMEM((slots, width, width), BF16),
            pltpu.VMEM((slots, width, width), BF16),
            pltpu.SMEM((1, slots), jnp.int32),
            pltpu.SMEM((1, slots), jnp.int32),
            pltpu.SMEM((1,), jnp.int32),
            pltpu.SMEM((1, 2), F32),
            pltpu.VMEM((iters, columns // n_row), F32),
            pltpu.VMEM((iters, rows), F32),
            pltpu.VMEM((iters, columns), jnp.int32),
            pltpu.VMEM((iters, rows), jnp.int32),
            pltpu.VMEM(z_shape[1:], F32),
            pltpu.VMEM(c_shape[1:], F32),
            pltpu.VMEM(z_shape[1:], F32),
            pltpu.VMEM(z_shape, F32),
            pltpu.VMEM(c_shape, F32),
            pltpu.VMEM((iters, zq, LANES), F32),
            pltpu.VMEM((iters,) + z_shape, jnp.int32),
            pltpu.VMEM((iters, cq, LANES), F32),
            pltpu.VMEM((iters * blocks, slots * width), BF16),
            pltpu.VMEM((slots, width), F32),
            pltpu.VMEM((slots, width), jnp.int32),
            pltpu.VMEM(z_shape, F32),
            pltpu.VMEM(z_shape, F32),
            pltpu.VMEM((iters,) + z_shape, F32),
            pltpu.VMEM((iters, n_row - 1, zq, LANES), F32),
            pltpu.VMEM((n_row, iters, zq, LANES), F32),
            pltpu.VMEM((n_row - 1, iters, zq, LANES), F32),
            pltpu.VMEM((iters,) + z_shape, F32),
            pltpu.VMEM((iters, n_row, slots, width), BF16),
            pltpu.VMEM((iters - 1,) + z_shape, F32),
            pltpu.VMEM((n_row, iters, zq, LANES), BF16),
            pltpu.VMEM(z_shape, F32),
            pltpu.VMEM((n_row, 1, 2 * LANES), F32),
            pltpu.VMEM((rows // LANES, LANES), F32),
            pltpu.VMEM((iters,) + c_shape, F32),
            pltpu.VMEM((iters, n_col - 1, cq, LANES), F32),
            pltpu.VMEM((iters - 1,) + c_shape, F32),
            pltpu.VMEM(z_shape, F32),
            pltpu.VMEM(c_shape[1:], F32),
            pltpu.VMEM((n_row, 1, LANES), F32),
            pltpu.VMEM((n_col, 1, LANES), F32),
            pltpu.VMEM((1, 2), F32),
            pltpu.SemaphoreType.DMA((14 + slots // 8,)),
            pltpu.SemaphoreType.DMA((phases,)),
            pltpu.SemaphoreType.DMA((phases,)),
        ],
        compiler_params=pltpu.CompilerParams(
            collective_id=0, has_side_effects=True, vmem_limit_bytes=64 << 20
        ),
        name="primal_dual_adjoint",
    )(
        tile_data.reshape(slots, width, width),
        tile_row_block.reshape(1, slots),
        tile_column_block.reshape(1, slots),
        tile_count.reshape(1),
        saved_primal,
        saved_dual,
        primal_mask,
        dual_mask,
        cost_vector.reshape(z_shape),
        demand.reshape(c_shape),
        upper_bound.reshape(z_shape),
        step_sizes.reshape(1, 2),
        primal_cotangent.reshape(z_shape),
        dual_cotangent.reshape(c_shape),
    )
    padj, dadj, grad = pl.pallas_call(
        hand_over,
        out_shape=tuple(jax.ShapeDtypeStruct(out.shape, F32) for out in outs),
        in_specs=[any_spec] * 3,
        out_specs=(any_spec,) * 3,
        scratch_shapes=[pltpu.VMEM(out.shape, F32) for out in outs] + [pltpu.SemaphoreType.DMA((6,))],
        compiler_params=pltpu.CompilerParams(vmem_limit_bytes=64 << 20),
        name="hand_over",
    )(*outs)
    return (padj.reshape(columns), dadj.reshape(rows // n_col), grad.reshape(2))


def solution(mesh):
    placed = (
        P("row", "col", None, None, None),
        P("row", "col", None),
        P("row", "col", None),
        P("row", "col"),
        P(None, "col"),
        P(None, "row"),
        P(None, "col"),
        P(None, "row"),
        P("col"),
        P("row"),
        P("col"),
        P(),
        P("col"),
        P("row"),
    )
    return jax.shard_map(
        local,
        mesh=mesh,
        in_specs=placed,
        out_specs=(P("col"), P(("row", "col")), P()),
        check_vma=False,
    )
```
